256 devices in a mesh: pair: 64 (over x, z, core), virt: 4 (over y).
Axes of the slice: x: 4, y: 4, z: 8, core: 2. Of those that a mesh axis runs over, the one named last changes fastest.
Arguments:
- amplitudes: bfloat16 [65536, 8, 1024], P('pair', 'virt'), may hold values from -6 to 6
- tile_mask: int32 [65536, 8], P('pair', 'virt'), may hold values from 0 to 1
- integrals: bfloat16 [8, 1024, 1024], P('virt', 'pair'), may hold values from -0.0625 to 0.0625
- pair_energy: float32 [65536], P(('pair', 'virt')), may hold values from -2 to -0.5
- virt_energy: float32 [1024], replicated, may hold values from 0.5 to 3
Outputs:
- update: bfloat16 [65536, 1024], P(('pair', 'virt'))
The draws below stay inside these ranges and needn't reach their ends.
All inputs are finite; a program needn't handle non-finite values.
Results may differ from the reference program's by a relative error of at most 0.011.
Values may be sent and summed in bfloat16 or wider, within the bound.
A program may use at most 64 MiB of HBM per device.

```python
import jax
import jax.numpy as jnp
from jax import lax

AB = 1024
CD = 1024
CD_DEV = 2
PAIR_DEV = 1024
NCD = 8
PAIRS = 65536


def draw_tile_mask(key, part):
    level = jax.random.randint(key, (PAIRS, NCD), 0, 4 * PAIRS)
    rising = PAIRS + 3 * jnp.arange(PAIRS, dtype=jnp.int32)[:, None]
    return (level < rising).astype(jnp.int32)


def level_of(stream_key, extent, cuts, smallest, largest):
    factor_of = 1.0
    for dim, parts in cuts:
        draws = jax.random.uniform(jax.random.fold_in(jax.random.fold_in(stream_key, 6), dim), (parts,), jnp.float32, smallest / len(cuts), largest / len(cuts))
        factor_of = factor_of * jnp.repeat(jnp.exp(draws), extent[dim] // parts).reshape((-1,) + (1,) * (len(extent) - 1 - dim))
    return factor_of


def centred(rng, dims, scale, bound, cuts=(), kind=jnp.bfloat16):
    entries = scale * jax.random.normal(rng, dims, jnp.float32)
    if cuts:
        entries = entries * level_of(rng, dims, cuts, -0.22, 0.18)
    return jnp.clip(entries, -bound, bound).astype(kind)


def setup_inputs(seed: int = 0) -> dict:
    arg_keys = jax.random.split(jax.random.key(seed), 6)
    return {
        "amplitudes": centred(arg_keys[0], (PAIRS, NCD, CD), 1.0, 6.0, ((0, 64), (1, 4))),
        "tile_mask": draw_tile_mask(jax.random.fold_in(arg_keys[5], 71), 0),
        "integrals": centred(arg_keys[2], (NCD, CD, AB), (NCD * CD) ** -0.5, 0.0625, ((0, 4), (1, 64))),
        "pair_energy": jnp.clip(-2.0 + 1.5 * jax.random.uniform(arg_keys[3], (PAIRS,), jnp.float32) ** level_of(arg_keys[3], (PAIRS,), ((0, 256),), -0.2, 0.2), -2.0, -0.5),
        "virt_energy": jnp.clip(jax.random.uniform(arg_keys[4], (AB,), jnp.float32, 0.5, 3.0), 0.5, 3.0),
    }


def reference(amplitudes, tile_mask, integrals, pair_energy, virt_energy):
    groups = NCD // CD_DEV
    masked = amplitudes * tile_mask.astype(jnp.bfloat16)[:, :, None]
    blocks = masked.reshape(PAIRS // PAIR_DEV, PAIR_DEV, NCD, CD)
    tiles = integrals.astype(jnp.float32)

    def one_block(block):
        fblock = block.astype(jnp.float32)
        total = jnp.zeros((PAIR_DEV, AB), jnp.float32)
        for group in range(groups):
            lo = group * CD_DEV
            part = jnp.einsum("ptk,tkn->pn", fblock[:, lo:lo + CD_DEV, :], tiles[lo:lo + CD_DEV])
            part = part.astype(jnp.bfloat16)
            part = lax.optimization_barrier(part)
            total = total + part.astype(jnp.float32)
        return total

    ladder = lax.map(one_block, blocks).reshape(PAIRS, AB)
    denom = virt_energy[None, :] - pair_energy[:, None]
    return (ladder / denom).astype(jnp.bfloat16)
```

```python
import functools

import jax
import jax.numpy as jnp
from jax import lax
from jax.experimental import pallas as pl
from jax.experimental.pallas import tpu as pltpu
from jax.sharding import PartitionSpec as P

MESH = pl.DeviceIdType.MESH
XN, ZN, KN, YN = 4, 8, 2, 4
W = 128
F32, BF16 = jnp.float32, jnp.bfloat16
ZGROUPS = ((0, 1), (1, 2), (2, 4), (4, 8))


def kernel(amp, mask, vin, pe, ve, out, xbuf, lhs, vb, perm, mb, pb, snd2, s_p, s_m,
           r2a, r2b, r_p, r_m, h_p, h_m, own, asem, vsem, zs, zr, xs, xr, cs, cr, ys, yr):
    pairs = lhs.shape[0]
    rows = pairs // YN
    half = rows // 2
    depth = vin.shape[1]
    chunks = vin.shape[2] // W
    kdim = XN * ZN * KN * depth

    me = lax.axis_index("pair")
    j = lax.axis_index("virt")
    k = me % KN
    z = (me // KN) % ZN
    x = me // (KN * ZN)

    def dev(xx, zz, kk):
        return {"pair": (xx * ZN + zz) * KN + kk, "virt": j}

    def ydev(jj):
        return {"pair": me, "virt": jj}

    xp, xm, xo = (x + 1) % XN, (x + XN - 1) % XN, (x + 2) % XN
    jp, jm, jo = (j + 1) % YN, (j + YN - 1) % YN, (j + 2) % YN
    partner = dev(x, z, 1 - k)
    zpeer = [dev(x, (z + d) % ZN, k) for d in range(ZN)]

    def remote(src, dst, ss, rs, to):
        return pltpu.make_async_remote_copy(
            src_ref=src, dst_ref=dst, send_sem=ss, recv_sem=rs, device_id=to, device_id_type=MESH)

    parts = asem.shape[0]
    part_rows = amp.shape[0] // parts

    def amp_copy(q):
        sl = pl.ds(q * part_rows, part_rows)
        return pltpu.make_async_copy(amp.at[sl], xbuf.at[sl], asem.at[q])

    for q in range(parts):
        amp_copy(q).start()
    own_copy = pltpu.make_async_copy(vin, vb.at[:, x, z, k], vsem)
    own_copy.start()

    barrier = pltpu.get_barrier_semaphore()
    friends = zpeer[1:] + [dev(xp, z, k), dev(xm, z, k), partner, ydev(jp), ydev(jm)]
    for to in friends:
        pl.semaphore_signal(barrier, inc=1, device_id=to, device_id_type=MESH)

    r = lax.broadcasted_iota(jnp.int32, (256, 256), 0)
    s = lax.broadcasted_iota(jnp.int32, (256, 256), 1)
    target = (r & 15) * 16 + ((r >> 4) & 7) * 2 + (r >> 7)
    perm[...] = jnp.where(s == target, 1.0, 0.0).astype(BF16)
    for t in range(2):
        row = mask[t:t + 1, :].astype(F32)
        mb[t] = jnp.broadcast_to(row, (128, pairs)).T
    pb[...] = jnp.broadcast_to(pe[...], (128, rows)).T

    pl.semaphore_wait(barrier, len(friends))

    def zcopy(g, d):
        lo, hi = ZGROUPS[g]
        cols = pl.ds(lo * W, (hi - lo) * W)
        return remote(vin.at[:, :, cols], vb.at[:, x, z, k, :, cols], zs.at[g, d], zr.at[g, d], zpeer[d])

    for g in range(len(ZGROUPS)):
        for d in (4, 3, 5, 2, 6, 1, 7):
            zcopy(g, d).start()

    def zwait(g):
        for d in range(1, ZN):
            zcopy(g, d).wait_recv()

    def column(xx, cols):
        return vb.at[:, xx, :, k, :, cols]

    def csl(c):
        return pl.ds(pl.multiple_of(c * W, W), W)

    def xcopy(c, way):
        cols = csl(c)
        if way == 0:
            return remote(column(x, cols), column(x, cols), xs.at[c, 0], xr.at[c, 0], dev(xp, z, k))
        if way == 1:
            return remote(column(x, cols), column(x, cols), xs.at[c, 1], xr.at[c, 1], dev(xm, z, k))
        if way == 2:
            ref = vb.at[0, xm, :, k, :, cols]
            return remote(ref, ref, xs.at[c, 2], xr.at[c, 2], dev(xp, z, k))
        ref = vb.at[1, xp, :, k, :, cols]
        return remote(ref, ref, xs.at[c, 3], xr.at[c, 3], dev(xm, z, k))

    def ccopy(c, n):
        ref = column((x, xm, xp, xo)[n], csl(c))
        return remote(ref, ref, cs.at[c, n], cr.at[c, n], partner)

    def g2(c):
        xcopy(c, 0).start()
        xcopy(c, 1).start()
        ccopy(c, 0).start()

    def g3(c):
        xcopy(c, 0).wait_recv()
        xcopy(c, 2).start()
        ccopy(c, 1).start()
        xcopy(c, 1).wait_recv()
        xcopy(c, 3).start()
        ccopy(c, 2).start()

    def g4(c):
        xcopy(c, 2).wait_recv()
        xcopy(c, 3).wait_recv()
        ccopy(c, 3).start()

    def gdone(c):
        for n in range(4):
            ccopy(c, n).wait_recv()

    def relayout(q):
        amp_copy(q).wait()
        steps = part_rows // 512

        @pl.loop(0, steps)
        def _(i):
            base = pl.multiple_of(q * part_rows + i * 512, 512)
            ab = jnp.concatenate([xbuf[pl.ds(base, 256), :], xbuf[pl.ds(base + 256, 256), :]], axis=1)
            res = jnp.dot(perm[...], ab, preferred_element_type=F32)
            for b in range(2):
                p0 = pl.multiple_of((q * part_rows) // 16 + i * 32 + b * 16, 16)
                for t in range(2):
                    m = mb[t, pl.ds(p0, 16), :]
                    for kt in range(8):
                        o = t * 128 + kt * 16
                        lhs[pl.ds(p0, 16), pl.ds(t * kdim + kt * 128, 128)] = (
                            res[o:o + 16, b * 128:b * 128 + 128] * m).astype(BF16)

    def ycopy(c, n):
        a, b = pl.ds(0, half), pl.ds(half, half)
        src, dst, to = (
            (snd2.at[c, a], r2a.at[c], jm),
            (snd2.at[c, b], r2b.at[c], jp),
            (s_p.at[c, a], r_m.at[c, a], jp),
            (s_m.at[c, b], r_p.at[c, b], jm),
            (s_p.at[c, b], r_m.at[c, b], jp),
            (s_m.at[c, a], r_p.at[c, a], jm),
        )[n]
        return remote(src, dst, ys.at[c, n], yr.at[c, n], ydev(to))

    def compute(c):
        cols = csl(c)
        rhs0 = vb[0, :, :, :, :, cols].reshape(kdim, W)
        rhs1 = vb[1, :, :, :, :, cols].reshape(kdim, W)

        def part(d):
            sl = pl.ds(pl.multiple_of(d * rows, rows), rows)
            return (jnp.dot(lhs[sl, 0:kdim], rhs0, preferred_element_type=F32)
                    + jnp.dot(lhs[sl, kdim:2 * kdim], rhs1, preferred_element_type=F32))

        snd2[c] = part(jo).astype(BF16)
        ycopy(c, 0).start()
        ycopy(c, 1).start()
        res = part(jp)
        s_p[c, 0:half] = res[0:half].astype(BF16)
        h_p[c % 2] = res[half:]
        ycopy(c, 2).start()
        res = part(jm)
        s_m[c, half:rows] = res[half:].astype(BF16)
        h_m[c % 2] = res[0:half]
        ycopy(c, 3).start()
        own[c % 3] = part(j)

    def combine(c):
        ycopy(c, 1).wait_recv()
        s_p[c, half:rows] = (h_p[c % 2] + r2b[c].astype(F32)).astype(BF16)
        ycopy(c, 4).start()
        ycopy(c, 0).wait_recv()
        s_m[c, 0:half] = (h_m[c % 2] + r2a[c].astype(F32)).astype(BF16)
        ycopy(c, 5).start()

    def final(c):
        for n in (2, 3, 4, 5):
            ycopy(c, n).wait_recv()
        cols = csl(c)
        total = own[c % 3] + r_p[c].astype(F32) + r_m[c].astype(F32)
        out[:, cols] = (total / (ve[:, cols] - pb[...])).astype(BF16)

    relayout(0)
    own_copy.wait()
    zwait(0)
    g2(0)
    relayout(1)
    zwait(1)
    g2(1)
    g3(0)
    relayout(2)
    zwait(2)
    g2(2)
    g4(0)
    g3(1)
    g2(3)
    relayout(3)

    @pl.loop(0, chunks)
    def _(c):
        gdone(c)

        compute(c)

        @pl.when(c + 1 < chunks)
        def _():
            g4(c + 1)

        @pl.when(c + 2 < chunks)
        def _():
            g3(c + 2)

        @pl.when(c == 0)
        def _():
            zwait(3)

        @pl.when(c + 4 < chunks)
        def _():
            g2(c + 4)

        @pl.when(c > 0)
        def _():
            combine(c - 1)

        @pl.when(c > 1)
        def _():
            final(c - 2)

    combine(chunks - 1)
    final(chunks - 2)
    final(chunks - 1)

    for g in range(len(ZGROUPS)):
        for d in range(1, ZN):
            zcopy(g, d).wait_send()

    @pl.loop(0, chunks)
    def _(c):
        for n in range(4):
            xcopy(c, n).wait_send()
            ccopy(c, n).wait_send()
        for n in range(6):
            ycopy(c, n).wait_send()


def on_device(amplitudes, tile_mask, integrals, pair_energy, virt_energy):
    pairs, tiles, kdim = amplitudes.shape
    depth, ab = integrals.shape[1:]
    rows = pairs // YN
    half = rows // 2
    chunks = ab // W
    kt = kdim // 128
    amp = amplitudes.reshape(pairs, tiles, kt, 128).transpose(0, 2, 1, 3).reshape(pairs * kt * tiles, 128)
    vmem = pl.BlockSpec(memory_space=pltpu.VMEM)
    dma = pltpu.SemaphoreType.DMA
    return pl.pallas_call(
        kernel,
        out_shape=jax.ShapeDtypeStruct((rows, ab), BF16),
        in_specs=[pl.BlockSpec(memory_space=pl.ANY), vmem, vmem, vmem, vmem],
        out_specs=vmem,
        scratch_shapes=[
            pltpu.VMEM(amp.shape, BF16),
            pltpu.VMEM((pairs, tiles * kdim), BF16),
            pltpu.VMEM((tiles, XN, ZN, KN, depth, ab), BF16),
            pltpu.VMEM((256, 256), BF16),
            pltpu.VMEM((tiles, pairs, 128), F32),
            pltpu.VMEM((rows, 128), F32),
            pltpu.VMEM((chunks, rows, W), BF16),
            pltpu.VMEM((chunks, rows, W), BF16),
            pltpu.VMEM((chunks, rows, W), BF16),
            pltpu.VMEM((chunks, half, W), BF16),
            pltpu.VMEM((chunks, half, W), BF16),
            pltpu.VMEM((chunks, rows, W), BF16),
            pltpu.VMEM((chunks, rows, W), BF16),
            pltpu.VMEM((2, half, W), F32),
            pltpu.VMEM((2, half, W), F32),
            pltpu.VMEM((3, rows, W), F32),
            dma((4,)),
            dma,
            dma((len(ZGROUPS), ZN)),
            dma((len(ZGROUPS), ZN)),
            dma((chunks, 4)),
            dma((chunks, 4)),
            dma((chunks, 4)),
            dma((chunks, 4)),
            dma((chunks, 6)),
            dma((chunks, 6)),
        ],
        compiler_params=pltpu.CompilerParams(collective_id=0, has_side_effects=True),
        name="ladder",
    )(amp, tile_mask.T, integrals, pair_energy[None, :], virt_energy[None, :])


def solution(mesh):
    placed = (
        P("pair", "virt", None),
        P("pair", "virt"),
        P("virt", "pair", None),
        P(("pair", "virt")),
        P(),
    )
    return jax.shard_map(
        on_device, mesh=mesh, in_specs=placed, out_specs=P(("pair", "virt"), None), check_vma=False
    )
```

```python
import functools

import jax
import jax.numpy as jnp
from jax import lax
from jax.experimental import pallas as pl
from jax.experimental.pallas import tpu as pltpu
from jax.sharding import PartitionSpec as P

MESH = pl.DeviceIdType.MESH
XN, ZN, KN, YN = 4, 8, 2, 4
W = 128
F32, BF16 = jnp.float32, jnp.bfloat16
GROUPS = ((0, 1, True), (1, 1, True), (2, 2, False), (4, 2, False), (6, 2, False))
NG = len(GROUPS)
PLAN = (
    ((0, 2),),
    ((2, 3), (3, 1), (4, 0), (1, 2)),
    ((2, 4), (3, 2), (4, 1), (2, 5), (2, 6)),
    ((3, 3), (4, 2)),
    ((3, 4), (4, 3), (3, 5), (3, 6)),
    ((4, 4),),
    ((4, 5), (4, 6)),
    (),
)
LAG, LAG2 = 2, 4


def kernel(amp, mask, vin, pe, ve, out, xbuf, lhs, vt, vb, perm, mb, pb, snd2, s_p, s_m,
           r2a, r2b, r_p, r_m, h_p, h_m, own, asem, tsem, vsem,
           es, er, qs, qr, ps, pr, ys, yr):
    pairs = lhs.shape[0]
    rows = pairs // YN
    half = rows // 2
    chunks, _, depth, _ = vt.shape
    kdim = XN * ZN * KN * depth

    me = lax.axis_index("pair")
    j = lax.axis_index("virt")
    k = me % KN
    z = (me // KN) % ZN
    x = me // (KN * ZN)

    def dev(dx, dz, kk):
        return {"pair": (((x + dx) % XN) * ZN + (z + dz) % ZN) * KN + kk, "virt": j}

    def ydev(jj):
        return {"pair": me, "virt": jj}

    def xa(d):
        return (x + d + XN) % XN

    def za(d):
        return (z + d + ZN) % ZN

    jp, jm, jo = (j + 1) % YN, (j + YN - 1) % YN, (j + 2) % YN
    partner = dev(0, 0, 1 - k)

    def remote(src, dst, ss, rs, to):
        return pltpu.make_async_remote_copy(
            src_ref=src, dst_ref=dst, send_sem=ss, recv_sem=rs, device_id=to, device_id_type=MESH)

    def same(ref, ss, rs, to):
        return remote(ref, ref, ss, rs, to)

    parts = asem.shape[0]
    part_rows = amp.shape[0] // parts

    def amp_copy(q):
        sl = pl.ds(q * part_rows, part_rows)
        return pltpu.make_async_copy(amp.at[sl], xbuf.at[sl], asem.at[q])

    def tile_copy(c):
        return pltpu.make_async_copy(vin.at[:, :, c * W:(c + 1) * W], vt.at[c], tsem.at[c])

    for c in range(chunks):
        tile_copy(c).start()
    for q in range(parts):
        amp_copy(q).start()

    barrier = pltpu.get_barrier_semaphore()
    friends = [dev(d, 0, kk) for d in range(1, XN) for kk in range(KN)]
    friends += [dev(0, d, kk) for d in range(1, ZN) for kk in range(KN)]
    friends += [partner, ydev(jp), ydev(jm)]
    for to in friends:
        pl.semaphore_signal(barrier, inc=1, device_id=to, device_id_type=MESH)

    for c in range(chunks):
        tile_copy(c).wait()
    own_copy = pltpu.make_async_copy(vt.at[:, k], vb.at[:, k, x, z, k], vsem)
    own_copy.start()

    r = lax.broadcasted_iota(jnp.int32, (256, 256), 0)
    s = lax.broadcasted_iota(jnp.int32, (256, 256), 1)
    target = (r & 15) * 16 + ((r >> 4) & 7) * 2 + (r >> 7)
    perm[...] = jnp.where(s == target, 1.0, 0.0).astype(BF16)
    for t in range(2):
        row = mask[t:t + 1, :].astype(F32)
        mb[t] = jnp.broadcast_to(row, (128, pairs)).T
    pb[...] = jnp.broadcast_to(pe[...], (128, rows)).T

    pl.semaphore_wait(barrier, len(friends))

    def gsl(g):
        return pl.ds(GROUPS[g][0], GROUPS[g][1])

    def first_x(g, d):
        return remote(vt.at[gsl(g), 0], vb.at[gsl(g), 0, x, z, k], es.at[g, d], er.at[g, d, k], dev(d, 0, 0))

    def first_z(g, d):
        return remote(vt.at[gsl(g), 1], vb.at[gsl(g), 1, x, z, k], es.at[g, 4 + d], er.at[g, d, k], dev(0, d, 1))

    def first_zd(g):
        return (4, 3, 5, 2, 6, 1, 7) if GROUPS[g][2] else (1, 7)

    def first_partner(g):
        return remote(vt.at[gsl(g), 1 - k], vb.at[gsl(g), 1 - k, x, z, k], es.at[g, 0], er.at[g, 0, k], partner)

    for g in range(NG):
        for d in first_zd(g):
            first_z(g, d).start()
        for d in (2, 1, 3):
            first_x(g, d).start()
        first_partner(g).start()

    def first_wait(g, ds):
        for d in ds:
            for kk in range(KN):
                remote(vt.at[gsl(g), 0], vb.at[gsl(g), 0, x, z, kk], es.at[g, d], er.at[g, d, kk], partner).wait_recv()
        remote(vt.at[gsl(g), 0], vb.at[gsl(g), 0, x, z, 0], es.at[g, 0], er.at[g, 0, 1 - k], partner).wait_recv()

    def row(g, dz, xs=slice(None)):
        return vb.at[gsl(g), 0, xs, za(dz)]

    def row_direct(g, d):
        return same(row(g, 0), qs.at[g, d], qr.at[g, d], dev(0, d, 0))

    def row_step(g, n, way):
        far = n == 3
        if way == 0:
            ref = row(g, -n, slice(0, XN // 2) if far else slice(None))
            return same(ref, qs.at[g, 2 * n], qr.at[g, 2 * n], dev(0, 1, 0))
        ref = row(g, n, slice(XN // 2, XN) if far else slice(None))
        return same(ref, qs.at[g, 2 * n + 1], qr.at[g, 2 * n + 1], dev(0, ZN - 1, 0))

    def row_partner(g, dz):
        return same(row(g, dz), ps.at[g, dz % ZN], pr.at[g, dz % ZN], partner)

    def ring_step(g, n, way):
        if way == 0:
            ref = vb.at[gsl(g), 1, x, za(-n)]
            return same(ref, qs.at[g, 2 * n - 2], qr.at[g, 2 * n - 2], dev(0, 1, 1))
        ref = vb.at[gsl(g), 1, x, za(n)]
        return same(ref, qs.at[g, 2 * n - 1], qr.at[g, 2 * n - 1], dev(0, ZN - 1, 1))

    def col(g, dx, zs=slice(None)):
        return vb.at[gsl(g), 1, xa(dx), zs]

    def col_direct(g, d):
        return same(col(g, 0), qs.at[g, 5 + d], qr.at[g, 5 + d], dev(d, 0, 1))

    def col_forward(g, way):
        if way == 0:
            return same(col(g, -1, slice(0, ZN // 2)), qs.at[g, 9], qr.at[g, 9], dev(1, 0, 1))
        return same(col(g, 1, slice(ZN // 2, ZN)), qs.at[g, 10], qr.at[g, 10], dev(XN - 1, 0, 1))

    def col_partner(g, dx):
        return same(col(g, dx), ps.at[g, dx % XN], pr.at[g, dx % XN], partner)

    def rows_all(g):
        if GROUPS[g][2]:
            return [row_direct(g, d) for d in (4, 3, 5, 2, 6, 1, 7)]
        return [row_step(g, n, w) for n in range(4) for w in range(2)]

    def cols_all(g):
        if GROUPS[g][2]:
            return [col_direct(g, d) for d in (2, 1, 3)]
        out = [ring_step(g, n, w) for n in (1, 2) for w in range(2)] + [ring_step(g, 3, 0)]
        return out + [col_direct(g, 1), col_direct(g, 3), col_forward(g, 0), col_forward(g, 1)]

    def stage_rows(g, st):
        direct = GROUPS[g][2]
        if st == 0:
            first_wait(g, (1, 2, 3))
            for cp in rows_all(g) if direct else (row_step(g, 0, 0), row_step(g, 0, 1)):
                cp.start()
            row_partner(g, 0).start()
        elif direct and st == 1:
            for d in (1, 7, 2, 6, 3, 5, 4):
                row_direct(g, d).wait_recv()
                row_partner(g, -d).start()
        elif not direct and st <= 3:
            row_step(g, st - 1, 0).wait_recv()
            row_step(g, st, 0).start()
            row_partner(g, -st).start()
            row_step(g, st - 1, 1).wait_recv()
            row_step(g, st, 1).start()
            row_partner(g, st).start()
        elif not direct and st == 4:
            row_step(g, 3, 0).wait_recv()
            row_step(g, 3, 1).wait_recv()
            row_partner(g, 4).start()
        elif st == (2 if direct else 6):
            for d in range(XN):
                col_partner(g, d).wait_recv()

    def stage_cols(g, st):
        direct = GROUPS[g][2]
        if st == 0:
            first_wait(g, range(1, ZN) if direct else (1, 7))
        if not direct and st <= 2:
            if st:
                ring_step(g, st, 0).wait_recv()
            ring_step(g, st + 1, 0).start()
            if st:
                ring_step(g, st, 1).wait_recv()
            if st < 2:
                ring_step(g, st + 1, 1).start()
        elif st == (0 if direct else 3):
            if not direct:
                ring_step(g, 3, 0).wait_recv()
            for d in (2, 1, 3) if direct else (1, 3):
                col_direct(g, d).start()
            col_partner(g, 0).start()
        elif direct and st == 1:
            for d in (1, 3, 2):
                col_direct(g, d).wait_recv()
                col_partner(g, -d).start()
        elif not direct and st == 4:
            col_direct(g, 1).wait_recv()
            col_forward(g, 0).start()
            col_partner(g, -1).start()
            col_direct(g, 3).wait_recv()
            col_forward(g, 1).start()
            col_partner(g, 1).start()
        elif not direct and st == 5:
            col_forward(g, 0).wait_recv()
            col_forward(g, 1).wait_recv()
            col_partner(g, 2).start()
        elif st == (2 if direct else 6):
            for d in range(ZN):
                row_partner(g, d).wait_recv()

    def stages(*steps):
        @pl.when(k == 0)
        def _():
            for g, st in steps:
                stage_rows(g, st)

        @pl.when(k == 1)
        def _():
            for g, st in steps:
                stage_cols(g, st)

    def relayout(q):
        amp_copy(q).wait()
        steps = part_rows // 512

        @pl.loop(0, steps)
        def _(i):
            base = pl.multiple_of(q * part_rows + i * 512, 512)
            ab = jnp.concatenate([xbuf[pl.ds(base, 256), :], xbuf[pl.ds(base + 256, 256), :]], axis=1)
            res = jnp.dot(perm[...], ab, preferred_element_type=F32)
            for b in range(2):
                p0 = pl.multiple_of((q * part_rows) // 16 + i * 32 + b * 16, 16)
                for t in range(2):
                    m = mb[t, pl.ds(p0, 16), :]
                    for kt in range(8):
                        o = t * 128 + kt * 16
                        lhs[pl.ds(p0, 16), pl.ds(t * kdim + kt * 128, 128)] = (
                            res[o:o + 16, b * 128:b * 128 + 128] * m).astype(BF16)

    def ycopy(c, n):
        a, b = pl.ds(0, half), pl.ds(half, half)
        src, dst, to = (
            (snd2.at[c, a], r2a.at[c], jm),
            (snd2.at[c, b], r2b.at[c], jp),
            (s_p.at[c, a], r_m.at[c, a], jp),
            (s_m.at[c, b], r_p.at[c, b], jm),
            (s_p.at[c, b], r_m.at[c, b], jp),
            (s_m.at[c, a], r_p.at[c, a], jm),
        )[n]
        return remote(src, dst, ys.at[c, n], yr.at[c, n], ydev(to))

    def compute(c):
        rhs0 = vb[c, 0].reshape(kdim, W)
        rhs1 = vb[c, 1].reshape(kdim, W)

        def part(d):
            sl = pl.ds(pl.multiple_of(d * rows, rows), rows)
            return (jnp.dot(lhs[sl, 0:kdim], rhs0, preferred_element_type=F32)
                    + jnp.dot(lhs[sl, kdim:2 * kdim], rhs1, preferred_element_type=F32))

        snd2[c] = part(jo).astype(BF16)
        ycopy(c, 0).start()
        ycopy(c, 1).start()
        res = part(jp)
        s_p[c, 0:half] = res[0:half].astype(BF16)
        h_p[c % (LAG + 1)] = res[half:]
        ycopy(c, 2).start()
        res = part(jm)
        s_m[c, half:rows] = res[half:].astype(BF16)
        h_m[c % (LAG + 1)] = res[0:half]
        ycopy(c, 3).start()
        own[c % (LAG2 + 1)] = part(j)

    def combine(c):
        ycopy(c, 1).wait_recv()
        s_p[c, half:rows] = (h_p[c % (LAG + 1)] + r2b[c].astype(F32)).astype(BF16)
        ycopy(c, 4).start()
        ycopy(c, 0).wait_recv()
        s_m[c, 0:half] = (h_m[c % (LAG + 1)] + r2a[c].astype(F32)).astype(BF16)
        ycopy(c, 5).start()

    def final(c):
        for n in (2, 3, 4, 5):
            ycopy(c, n).wait_recv()
        cols = pl.ds(pl.multiple_of(c * W, W), W)
        total = own[c % (LAG2 + 1)] + r_p[c].astype(F32) + r_m[c].astype(F32)
        out[:, cols] = (total / (ve[:, cols] - pb[...])).astype(BF16)

    relayout(0)
    own_copy.wait()
    relayout(1)
    stages((0, 0), (1, 0))
    relayout(2)
    stages((2, 0), (0, 1))
    relayout(3)
    stages((2, 1), (1, 1), (2, 2), (3, 0))

    @pl.loop(0, chunks)
    def _(c):
        for cc, steps in enumerate(PLAN):
            if steps:
                @pl.when(c == cc)
                def _():
                    stages(*steps)

        compute(c)

        @pl.when(c >= LAG)
        def _():
            combine(c - LAG)

        @pl.when(c >= LAG2)
        def _():
            final(c - LAG2)

    for n in range(LAG, 0, -1):
        combine(chunks - n)
    for n in range(LAG2, 0, -1):
        final(chunks - n)

    for g in range(NG):
        for d in first_zd(g):
            first_z(g, d).wait_send()
        for d in (1, 2, 3):
            first_x(g, d).wait_send()
        first_partner(g).wait_send()

    @pl.when(k == 0)
    def _():
        for g in range(NG):
            for cp in rows_all(g) + [row_partner(g, d) for d in range(ZN)]:
                cp.wait_send()

    @pl.when(k == 1)
    def _():
        for g in range(NG):
            for cp in cols_all(g) + [col_partner(g, d) for d in range(XN)]:
                cp.wait_send()

    @pl.loop(0, chunks)
    def _(c):
        for n in range(6):
            ycopy(c, n).wait_send()


def on_device(amplitudes, tile_mask, integrals, pair_energy, virt_energy):
    pairs, tiles, kdim = amplitudes.shape
    depth, ab = integrals.shape[1:]
    rows = pairs // YN
    half = rows // 2
    chunks = ab // W
    kt = kdim // 128
    amp = amplitudes.reshape(pairs, tiles, kt, 128).transpose(0, 2, 1, 3).reshape(pairs * kt * tiles, 128)
    vmem = pl.BlockSpec(memory_space=pltpu.VMEM)
    dma = pltpu.SemaphoreType.DMA
    return pl.pallas_call(
        kernel,
        out_shape=jax.ShapeDtypeStruct((rows, ab), BF16),
        in_specs=[pl.BlockSpec(memory_space=pl.ANY), vmem, pl.BlockSpec(memory_space=pl.ANY), vmem, vmem],
        out_specs=vmem,
        scratch_shapes=[
            pltpu.VMEM(amp.shape, BF16),
            pltpu.VMEM((pairs, tiles * kdim), BF16),
            pltpu.VMEM((chunks, tiles, depth, W), BF16),
            pltpu.VMEM((chunks, tiles, XN, ZN, KN, depth, W), BF16),
            pltpu.VMEM((256, 256), BF16),
            pltpu.VMEM((tiles, pairs, 128), F32),
            pltpu.VMEM((rows, 128), F32),
            pltpu.VMEM((chunks, rows, W), BF16),
            pltpu.VMEM((chunks, rows, W), BF16),
            pltpu.VMEM((chunks, rows, W), BF16),
            pltpu.VMEM((chunks, half, W), BF16),
            pltpu.VMEM((chunks, half, W), BF16),
            pltpu.VMEM((chunks, rows, W), BF16),
            pltpu.VMEM((chunks, rows, W), BF16),
            pltpu.VMEM((LAG + 1, half, W), F32),
            pltpu.VMEM((LAG + 1, half, W), F32),
            pltpu.VMEM((LAG2 + 1, rows, W), F32),
            dma((4,)),
            dma((chunks,)),
            dma,
            dma((NG, 12)),
            dma((NG, ZN, KN)),
            dma((NG, 11)),
            dma((NG, 11)),
            dma((NG, ZN)),
            dma((NG, ZN)),
            dma((chunks, 6)),
            dma((chunks, 6)),
        ],
        compiler_params=pltpu.CompilerParams(collective_id=0, has_side_effects=True),
        name="ladder",
    )(amp, tile_mask.T, integrals, pair_energy[None, :], virt_energy[None, :])


def solution(mesh):
    placed = (
        P("pair", "virt", None),
        P("pair", "virt"),
        P("virt", "pair", None),
        P(("pair", "virt")),
        P(),
    )
    return jax.shard_map(
        on_device, mesh=mesh, in_specs=placed, out_specs=P(("pair", "virt"), None), check_vma=False
    )
```

```python
import functools

import jax
import jax.numpy as jnp
from jax import lax
from jax.experimental import pallas as pl
from jax.experimental.pallas import tpu as pltpu
from jax.sharding import PartitionSpec as P

MESH = pl.DeviceIdType.MESH
XN, ZN, KN, YN = 4, 8, 2, 4
W = 128
F32, BF16 = jnp.float32, jnp.bfloat16
NP = 3
FIRST = ((0, 1), (1, 2))
GROUPS = ((3, 2, False), (5, 3, False))
NG = len(GROUPS)
PRE = (
    (),
    (),
    (),
    (('Q', 0, 0), ('Q', 1, 0), ('P', 0, 0), ('P', 1, 0), ('P', 2, 0), ('Q', 0, 1), ('P', 0, 1), ('Q', 1, 1), ('P', 1, 1), ('P', 0, 2), ('Q', 0, 2), ('Q', 1, 2), ('P', 2, 1)),
)
PLAN = (
    ((('P', 0, 3),), (('P', 1, 2),), (), (('Q', 0, 3),)),
    ((('Q', 1, 3), ('P', 1, 3)), (('P', 2, 2),), (), ()),
    ((('P', 2, 3),), (('Q', 0, 4), ('Q', 1, 4)), (), ()),
    ((('Q', 0, 5), ('Q', 0, 6)), (), (), (('Q', 1, 5),)),
    ((), (), (), ()),
    ((('Q', 1, 6),), (), (), ()),
    ((), (), (), ()),
    ((), (), (), ()),
)
LAG, LAG2 = 2, 4


def kernel(amp, mask, vin, pe, ve, out, xbuf, lhs, vt, vb, perm, mb, pb, snd2, s_p, s_m,
           r2a, r2b, r_p, r_m, h_p, h_m, own, asem, tsem, vsem,
           fs, fr, cs, cr, ks, kr, es, er, qs, qr, ps, pr, ys, yr):
    pairs = lhs.shape[0]
    rows = pairs // YN
    half = rows // 2
    chunks, _, depth, _ = vt.shape
    kdim = XN * ZN * KN * depth

    me = lax.axis_index("pair")
    j = lax.axis_index("virt")
    k = me % KN
    z = (me // KN) % ZN
    x = me // (KN * ZN)

    def dev(dx, dz, kk):
        return {"pair": (((x + dx) % XN) * ZN + (z + dz) % ZN) * KN + kk, "virt": j}

    def ydev(jj):
        return {"pair": me, "virt": jj}

    def xa(d):
        return (x + d + XN) % XN

    def za(d):
        return (z + d + ZN) % ZN

    jp, jm, jo = (j + 1) % YN, (j + YN - 1) % YN, (j + 2) % YN
    partner = dev(0, 0, 1 - k)

    def remote(src, dst, ss, rs, to):
        return pltpu.make_async_remote_copy(
            src_ref=src, dst_ref=dst, send_sem=ss, recv_sem=rs, device_id=to, device_id_type=MESH)

    def same(ref, ss, rs, to):
        return remote(ref, ref, ss, rs, to)

    parts = asem.shape[0]
    part_rows = amp.shape[0] // parts

    def amp_copy(q):
        sl = pl.ds(q * part_rows, part_rows)
        return pltpu.make_async_copy(amp.at[sl], xbuf.at[sl], asem.at[q])

    def tile_copy(c):
        return pltpu.make_async_copy(vin.at[:, :, c * W:(c + 1) * W], vt.at[c], tsem.at[c])

    for c in range(chunks):
        tile_copy(c).start()
    for q in range(parts):
        amp_copy(q).start()

    barrier = pltpu.get_barrier_semaphore()
    friends = [dev(d, 0, kk) for d in range(1, XN) for kk in range(KN)]
    friends += [dev(0, d, kk) for d in range(1, ZN) for kk in range(KN)]
    friends += [partner, ydev(jp), ydev(jm)]
    for to in friends:
        pl.semaphore_signal(barrier, inc=1, device_id=to, device_id_type=MESH)

    for c in range(chunks):
        tile_copy(c).wait()
    own_copy = pltpu.make_async_copy(vt.at[:, k], vb.at[:, k, x, z, k], vsem)
    own_copy.start()

    r = lax.broadcasted_iota(jnp.int32, (256, 256), 0)
    s = lax.broadcasted_iota(jnp.int32, (256, 256), 1)
    target = (r & 15) * 16 + ((r >> 4) & 7) * 2 + (r >> 7)
    perm[...] = jnp.where(s == target, 1.0, 0.0).astype(BF16)
    for t in range(2):
        row = mask[t:t + 1, :].astype(F32)
        mb[t] = jnp.broadcast_to(row, (128, pairs)).T
    pb[...] = jnp.broadcast_to(pe[...], (128, rows)).T

    def relayout(q):
        amp_copy(q).wait()
        steps = part_rows // 512

        @pl.loop(0, steps)
        def _(i):
            base = pl.multiple_of(q * part_rows + i * 512, 512)
            ab = jnp.concatenate([xbuf[pl.ds(base, 256), :], xbuf[pl.ds(base + 256, 256), :]], axis=1)
            res = jnp.dot(perm[...], ab, preferred_element_type=F32)
            for b in range(2):
                p0 = pl.multiple_of((q * part_rows) // 16 + i * 32 + b * 16, 16)
                for t in range(2):
                    m = mb[t, pl.ds(p0, 16), :]
                    for kt in range(8):
                        o = t * 128 + kt * 16
                        lhs[pl.ds(p0, 16), pl.ds(t * kdim + kt * 128, 128)] = (
                            res[o:o + 16, b * 128:b * 128 + 128] * m).astype(BF16)

    relayout(0)
    pl.semaphore_wait(barrier, len(friends))

    def gsl(g):
        return pl.ds(GROUPS[g][0], GROUPS[g][1])

    def first_x(g, d):
        return remote(vt.at[gsl(g), 0], vb.at[gsl(g), 0, x, z, k], es.at[g, d], er.at[g, d, k], dev(d, 0, 0))

    def first_z(g, d):
        return remote(vt.at[gsl(g), 1], vb.at[gsl(g), 1, x, z, k], es.at[g, 4 + d], er.at[g, d, k], dev(0, d, 1))

    def first_zd(g):
        return (4, 3, 5, 2, 6, 1, 7) if GROUPS[g][2] else (1, 7)

    def first_partner(g):
        return remote(vt.at[gsl(g), 1 - k], vb.at[gsl(g), 1 - k, x, z, k], es.at[g, 0], er.at[g, 0, k], partner)

    def fsl(f):
        return pl.ds(FIRST[f][0], FIRST[f][1])

    def p_first(f, d, t):
        return remote(vt.at[fsl(f), t], vb.at[fsl(f), t, x, z, k], fs.at[f, d, t], fr.at[f, d, k], dev(0, d, t))

    def p_partner_first(f):
        return remote(vt.at[fsl(f), 1 - k], vb.at[fsl(f), 1 - k, x, z, k], fs.at[f, 0, 0], fr.at[f, 0, k], partner)

    def p_first_wait(f):
        def got(d, kk):
            remote(vt.at[fsl(f), 0], vb.at[fsl(f), k, x, za(-d), kk], fs.at[f, d, 0], fr.at[f, d, kk], partner).wait_recv()

        for d in range(1, ZN):
            for kk in range(KN):
                got(d, kk)
        got(0, 1 - k)

    def p_col(c, dx, zs=slice(None)):
        return vb.at[c, k, xa(dx), zs]

    def p_x(c, n):
        if n < 2:
            return same(p_col(c, 0), cs.at[c, n], cr.at[c, n], dev((1, XN - 1)[n], 0, k))
        if n == 2:
            return same(p_col(c, -1, slice(0, ZN // 2)), cs.at[c, 2], cr.at[c, 2], dev(1, 0, k))
        return same(p_col(c, 1, slice(ZN // 2, ZN)), cs.at[c, 3], cr.at[c, 3], dev(XN - 1, 0, k))

    def p_partner(c, dx):
        return same(p_col(c, dx), ks.at[c, dx % XN], kr.at[c, dx % XN], partner)

    def p_stage(c, st):
        if st == 0:
            for f, (c0, _) in enumerate(FIRST):
                if c == c0:
                    p_first_wait(f)
            p_x(c, 0).start()
            p_x(c, 1).start()
            p_partner(c, 0).start()
        elif st == 1:
            for n, dx in ((0, -1), (1, 1)):
                p_x(c, n).wait_recv()
                p_x(c, n + 2).start()
                p_partner(c, dx).start()
        elif st == 2:
            p_x(c, 2).wait_recv()
            p_x(c, 3).wait_recv()
            p_partner(c, 2).start()
        else:
            for d in range(XN):
                p_partner(c, d).wait_recv()

    def start_p(f):
        for d in (4, 3, 5, 2, 6, 1, 7):
            for t in range(2):
                p_first(f, d, t).start()
        p_partner_first(f).start()

    start_p(0)
    for g in range(NG):
        for d in first_zd(g):
            first_z(g, d).start()
        for d in (2, 1, 3):
            first_x(g, d).start()
        first_partner(g).start()
    for f in range(1, len(FIRST)):
        start_p(f)

    def first_wait(g, ds):
        for d in ds:
            for kk in range(KN):
                remote(vt.at[gsl(g), 0], vb.at[gsl(g), 0, x, z, kk], es.at[g, d], er.at[g, d, kk], partner).wait_recv()
        remote(vt.at[gsl(g), 0], vb.at[gsl(g), 0, x, z, 0], es.at[g, 0], er.at[g, 0, 1 - k], partner).wait_recv()

    def row(g, dz, xs=slice(None)):
        return vb.at[gsl(g), 0, xs, za(dz)]

    def row_direct(g, d):
        return same(row(g, 0), qs.at[g, d], qr.at[g, d], dev(0, d, 0))

    def row_step(g, n, way):
        far = n == 3
        if way == 0:
            ref = row(g, -n, slice(0, XN // 2) if far else slice(None))
            return same(ref, qs.at[g, 2 * n], qr.at[g, 2 * n], dev(0, 1, 0))
        ref = row(g, n, slice(XN // 2, XN) if far else slice(None))
        return same(ref, qs.at[g, 2 * n + 1], qr.at[g, 2 * n + 1], dev(0, ZN - 1, 0))

    def row_partner(g, dz):
        return same(row(g, dz), ps.at[g, dz % ZN], pr.at[g, dz % ZN], partner)

    def ring_step(g, n, way):
        if way == 0:
            ref = vb.at[gsl(g), 1, x, za(-n)]
            return same(ref, qs.at[g, 2 * n - 2], qr.at[g, 2 * n - 2], dev(0, 1, 1))
        ref = vb.at[gsl(g), 1, x, za(n)]
        return same(ref, qs.at[g, 2 * n - 1], qr.at[g, 2 * n - 1], dev(0, ZN - 1, 1))

    def col(g, dx, zs=slice(None)):
        return vb.at[gsl(g), 1, xa(dx), zs]

    def col_direct(g, d):
        return same(col(g, 0), qs.at[g, 5 + d], qr.at[g, 5 + d], dev(d, 0, 1))

    def col_forward(g, way):
        if way == 0:
            return same(col(g, -1, slice(0, ZN // 2)), qs.at[g, 9], qr.at[g, 9], dev(1, 0, 1))
        return same(col(g, 1, slice(ZN // 2, ZN)), qs.at[g, 10], qr.at[g, 10], dev(XN - 1, 0, 1))

    def col_partner(g, dx):
        return same(col(g, dx), ps.at[g, dx % XN], pr.at[g, dx % XN], partner)

    def rows_all(g):
        if GROUPS[g][2]:
            return [row_direct(g, d) for d in (4, 3, 5, 2, 6, 1, 7)]
        return [row_step(g, n, w) for n in range(4) for w in range(2)]

    def cols_all(g):
        if GROUPS[g][2]:
            return [col_direct(g, d) for d in (2, 1, 3)]
        out = [ring_step(g, n, w) for n in (1, 2) for w in range(2)] + [ring_step(g, 3, 0)]
        return out + [col_direct(g, 1), col_direct(g, 3), col_forward(g, 0), col_forward(g, 1)]

    def stage_rows(g, st):
        direct = GROUPS[g][2]
        if st == 0:
            first_wait(g, (1, 2, 3))
            for cp in rows_all(g) if direct else (row_step(g, 0, 0), row_step(g, 0, 1)):
                cp.start()
            row_partner(g, 0).start()
        elif direct and st == 1:
            for d in (1, 7, 2, 6, 3, 5, 4):
                row_direct(g, d).wait_recv()
                row_partner(g, -d).start()
        elif not direct and st <= 3:
            row_step(g, st - 1, 0).wait_recv()
            row_step(g, st, 0).start()
            row_partner(g, -st).start()
            row_step(g, st - 1, 1).wait_recv()
            row_step(g, st, 1).start()
            row_partner(g, st).start()
        elif not direct and st == 4:
            row_step(g, 3, 0).wait_recv()
            row_step(g, 3, 1).wait_recv()
            row_partner(g, 4).start()
        elif st == (2 if direct else 6):
            for d in range(XN):
                col_partner(g, d).wait_recv()

    def stage_cols(g, st):
        direct = GROUPS[g][2]
        if st == 0:
            first_wait(g, range(1, ZN) if direct else (1, 7))
        if not direct and st <= 2:
            if st:
                ring_step(g, st, 0).wait_recv()
            ring_step(g, st + 1, 0).start()
            if st:
                ring_step(g, st, 1).wait_recv()
            if st < 2:
                ring_step(g, st + 1, 1).start()
        elif st == (0 if direct else 3):
            if not direct:
                ring_step(g, 3, 0).wait_recv()
            for d in (2, 1, 3) if direct else (1, 3):
                col_direct(g, d).start()
            col_partner(g, 0).start()
        elif direct and st == 1:
            for d in (1, 3, 2):
                col_direct(g, d).wait_recv()
                col_partner(g, -d).start()
        elif not direct and st == 4:
            col_direct(g, 1).wait_recv()
            col_forward(g, 0).start()
            col_partner(g, -1).start()
            col_direct(g, 3).wait_recv()
            col_forward(g, 1).start()
            col_partner(g, 1).start()
        elif not direct and st == 5:
            col_forward(g, 0).wait_recv()
            col_forward(g, 1).wait_recv()
            col_partner(g, 2).start()
        elif st == (2 if direct else 6):
            for d in range(ZN):
                row_partner(g, d).wait_recv()

    def stages(steps):
        for kind, n, st in steps:
            if kind == "P":
                p_stage(n, st)
            else:
                @pl.when(k == 0)
                def _():
                    stage_rows(n, st)

                @pl.when(k == 1)
                def _():
                    stage_cols(n, st)

    def ycopy(c, n):
        a, b = pl.ds(0, half), pl.ds(half, half)
        src, dst, to = (
            (snd2.at[c, a], r2a.at[c], jm),
            (snd2.at[c, b], r2b.at[c], jp),
            (s_p.at[c, a], r_m.at[c, a], jp),
            (s_m.at[c, b], r_p.at[c, b], jm),
            (s_p.at[c, b], r_m.at[c, b], jp),
            (s_m.at[c, a], r_p.at[c, a], jm),
        )[n]
        return remote(src, dst, ys.at[c, n], yr.at[c, n], ydev(to))

    def compute(c, slot):

        def part(d):
            sl = pl.ds(pl.multiple_of(d * rows, rows), rows)
            rhs0 = vb[c, 0].reshape(kdim, W)
            rhs1 = vb[c, 1].reshape(kdim, W)
            return (jnp.dot(lhs[sl, 0:kdim], rhs0, preferred_element_type=F32)
                    + jnp.dot(lhs[sl, kdim:2 * kdim], rhs1, preferred_element_type=F32))

        slot(0)
        snd2[c] = part(jo).astype(BF16)
        ycopy(c, 0).start()
        ycopy(c, 1).start()
        slot(1)
        res = part(jp)
        s_p[c, 0:half] = res[0:half].astype(BF16)
        h_p[c % (LAG + 1)] = res[half:]
        ycopy(c, 2).start()
        slot(2)
        res = part(jm)
        s_m[c, half:rows] = res[half:].astype(BF16)
        h_m[c % (LAG + 1)] = res[0:half]
        ycopy(c, 3).start()
        slot(3)
        own[c % (LAG2 + 1)] = part(j)

    def combine(c):
        ycopy(c, 1).wait_recv()
        s_p[c, half:rows] = (h_p[c % (LAG + 1)] + r2b[c].astype(F32)).astype(BF16)
        ycopy(c, 4).start()
        ycopy(c, 0).wait_recv()
        s_m[c, 0:half] = (h_m[c % (LAG + 1)] + r2a[c].astype(F32)).astype(BF16)
        ycopy(c, 5).start()

    def final(c):
        for n in (2, 3, 4, 5):
            ycopy(c, n).wait_recv()
        cols = pl.ds(pl.multiple_of(c * W, W), W)
        total = own[c % (LAG2 + 1)] + r_p[c].astype(F32) + r_m[c].astype(F32)
        out[:, cols] = (total / (ve[:, cols] - pb[...])).astype(BF16)

    own_copy.wait()
    stages(PRE[0])
    for q in range(1, parts):
        relayout(q)
        stages(PRE[q])

    @pl.loop(0, chunks)
    def _(c):
        def slot(n):
            for cc, slots in enumerate(PLAN):
                if slots[n]:
                    @pl.when(c == cc)
                    def _():
                        stages(slots[n])

        compute(c, slot)

        @pl.when(c >= LAG)
        def _():
            combine(c - LAG)

        @pl.when(c >= LAG2)
        def _():
            final(c - LAG2)

    for n in range(LAG, 0, -1):
        combine(chunks - n)
    for n in range(LAG2, 0, -1):
        final(chunks - n)

    for g in range(NG):
        for d in first_zd(g):
            first_z(g, d).wait_send()
        for d in (1, 2, 3):
            first_x(g, d).wait_send()
        first_partner(g).wait_send()
    for f in range(len(FIRST)):
        for d in range(1, ZN):
            for t in range(2):
                p_first(f, d, t).wait_send()
        p_partner_first(f).wait_send()

    @pl.loop(0, NP)
    def _(c):
        for n in range(4):
            p_x(c, n).wait_send()
            p_partner(c, n).wait_send()

    @pl.when(k == 0)
    def _():
        for g in range(NG):
            for cp in rows_all(g) + [row_partner(g, d) for d in range(ZN)]:
                cp.wait_send()

    @pl.when(k == 1)
    def _():
        for g in range(NG):
            for cp in cols_all(g) + [col_partner(g, d) for d in range(XN)]:
                cp.wait_send()

    @pl.loop(0, chunks)
    def _(c):
        for n in range(6):
            ycopy(c, n).wait_send()


def on_device(amplitudes, tile_mask, integrals, pair_energy, virt_energy):
    pairs, tiles, kdim = amplitudes.shape
    depth, ab = integrals.shape[1:]
    rows = pairs // YN
    half = rows // 2
    chunks = ab // W
    kt = kdim // 128
    amp = amplitudes.reshape(pairs, tiles, kt, 128).transpose(0, 2, 1, 3).reshape(pairs * kt * tiles, 128)
    vmem = pl.BlockSpec(memory_space=pltpu.VMEM)
    dma = pltpu.SemaphoreType.DMA
    return pl.pallas_call(
        kernel,
        out_shape=jax.ShapeDtypeStruct((rows, ab), BF16),
        in_specs=[pl.BlockSpec(memory_space=pl.ANY), vmem, pl.BlockSpec(memory_space=pl.ANY), vmem, vmem],
        out_specs=vmem,
        scratch_shapes=[
            pltpu.VMEM(amp.shape, BF16),
            pltpu.VMEM((pairs, tiles * kdim), BF16),
            pltpu.VMEM((chunks, tiles, depth, W), BF16),
            pltpu.VMEM((chunks, tiles, XN, ZN, KN, depth, W), BF16),
            pltpu.VMEM((256, 256), BF16),
            pltpu.VMEM((tiles, pairs, 128), F32),
            pltpu.VMEM((rows, 128), F32),
            pltpu.VMEM((chunks, rows, W), BF16),
            pltpu.VMEM((chunks, rows, W), BF16),
            pltpu.VMEM((chunks, rows, W), BF16),
            pltpu.VMEM((chunks, half, W), BF16),
            pltpu.VMEM((chunks, half, W), BF16),
            pltpu.VMEM((chunks, rows, W), BF16),
            pltpu.VMEM((chunks, rows, W), BF16),
            pltpu.VMEM((LAG + 1, half, W), F32),
            pltpu.VMEM((LAG + 1, half, W), F32),
            pltpu.VMEM((LAG2 + 1, rows, W), F32),
            dma((4,)),
            dma((chunks,)),
            dma,
            dma((len(FIRST), ZN, KN)),
            dma((len(FIRST), ZN, KN)),
            dma((NP, 4)),
            dma((NP, 4)),
            dma((NP, 4)),
            dma((NP, 4)),
            dma((NG, 12)),
            dma((NG, ZN, KN)),
            dma((NG, 11)),
            dma((NG, 11)),
            dma((NG, ZN)),
            dma((NG, ZN)),
            dma((chunks, 6)),
            dma((chunks, 6)),
        ],
        compiler_params=pltpu.CompilerParams(collective_id=0, has_side_effects=True),
        name="ladder",
    )(amp, tile_mask.T, integrals, pair_energy[None, :], virt_energy[None, :])


def solution(mesh):
    placed = (
        P("pair", "virt", None),
        P("pair", "virt"),
        P("virt", "pair", None),
        P(("pair", "virt")),
        P(),
    )
    return jax.shard_map(
        on_device, mesh=mesh, in_specs=placed, out_specs=P(("pair", "virt"), None), check_vma=False
    )
```

```python
import functools

import jax
import jax.numpy as jnp
from jax import lax
from jax.experimental import pallas as pl
from jax.experimental.pallas import tpu as pltpu
from jax.sharding import PartitionSpec as P

MESH = pl.DeviceIdType.MESH
XN, ZN, KN, YN = 4, 8, 2, 4
W = 128
F32, BF16 = jnp.float32, jnp.bfloat16
NP = 3
FIRST = ((0, 1), (1, 2))
GROUPS = ((3, 2, False), (5, 3, False))
NG = len(GROUPS)
PRE = (
    (),
    (),
    (),
    (('Q', 0, 0), ('Q', 1, 0), ('P', 0, 0), ('P', 1, 0), ('P', 2, 0), ('Q', 0, 1), ('P', 0, 1), ('Q', 1, 1), ('P', 1, 1), ('P', 0, 2), ('Q', 0, 2), ('Q', 1, 2), ('P', 2, 1)),
)
BLOCKS = ((0, 1), (1, 1), (2, 1), (3, 2), (5, 2), (7, 1))
PLAN = (
    ((('P', 0, 3),), (('P', 1, 2),), (), (('Q', 0, 3),)),
    ((('Q', 1, 3), ('P', 1, 3)), (('P', 2, 2),), (), ()),
    ((('P', 2, 3),), (('Q', 0, 4), ('Q', 1, 4)), (), ()),
    ((('Q', 0, 5), ('Q', 0, 6)), (), (), (('Q', 1, 5),)),
    ((('Q', 1, 6),), (), (), ()),
    ((), (), (), ()),
)
NB = len(BLOCKS)
LAG, LAG2 = 1, 3


def kernel(amp, mask_in, vin, pe_in, ve_in, out, mask, pe, ve, xbuf, lhs, vt, vb, perm, mb, pb, snd2, s_p, s_m,
           r2a, r2b, r_p, r_m, h_p, h_m, own, asem, tsem, isem, vsem,
           fs, fr, cs, cr, ks, kr, es, er, qs, qr, ps, pr, ys, yr):
    pairs = lhs.shape[0]
    rows = pairs // YN
    half = rows // 2
    chunks, _, depth, _ = vt.shape
    kdim = XN * ZN * KN * depth

    me = lax.axis_index("pair")
    j = lax.axis_index("virt")
    k = me % KN
    z = (me // KN) % ZN
    x = me // (KN * ZN)

    def dev(dx, dz, kk):
        return {"pair": (((x + dx) % XN) * ZN + (z + dz) % ZN) * KN + kk, "virt": j}

    def ydev(jj):
        return {"pair": me, "virt": jj}

    def xa(d):
        return (x + d + XN) % XN

    def za(d):
        return (z + d + ZN) % ZN

    jp, jm, jo = (j + 1) % YN, (j + YN - 1) % YN, (j + 2) % YN
    partner = dev(0, 0, 1 - k)

    def remote(src, dst, ss, rs, to):
        return pltpu.make_async_remote_copy(
            src_ref=src, dst_ref=dst, send_sem=ss, recv_sem=rs, device_id=to, device_id_type=MESH)

    def same(ref, ss, rs, to):
        return remote(ref, ref, ss, rs, to)

    parts = asem.shape[0]
    part_rows = amp.shape[0] // parts

    def amp_copy(q):
        sl = pl.ds(q * part_rows, part_rows)
        return pltpu.make_async_copy(amp.at[sl], xbuf.at[sl], asem.at[q])

    def tile_copy(c):
        return pltpu.make_async_copy(vin.at[:, :, c * W:(c + 1) * W], vt.at[c], tsem.at[c])

    barrier = pltpu.get_barrier_semaphore()
    friends = [dev(d, 0, kk) for d in range(1, XN) for kk in range(KN)]
    friends += [dev(0, d, kk) for d in range(1, ZN) for kk in range(KN)]
    friends += [partner, ydev(jp), ydev(jm)]
    for to in friends:
        pl.semaphore_signal(barrier, inc=1, device_id=to, device_id_type=MESH)

    for c in range(chunks):
        tile_copy(c).start()
    for q in range(parts):
        amp_copy(q).start()
    small = [pltpu.make_async_copy(src, dst, isem.at[i])
             for i, (src, dst) in enumerate(((mask_in, mask), (pe_in, pe), (ve_in, ve)))]
    for cp in small:
        cp.start()
    for c in range(chunks):
        tile_copy(c).wait()
    own_copy = pltpu.make_async_copy(vt.at[:, k], vb.at[:, k, x, z, k], vsem)
    own_copy.start()

    r = lax.broadcasted_iota(jnp.int32, (256, 256), 0)
    s = lax.broadcasted_iota(jnp.int32, (256, 256), 1)
    target = (r & 15) * 16 + ((r >> 4) & 7) * 2 + (r >> 7)
    perm[...] = jnp.where(s == target, 1.0, 0.0).astype(BF16)
    for cp in small:
        cp.wait()
    for t in range(2):
        row = mask[t:t + 1, :].astype(F32)
        mb[t] = jnp.broadcast_to(row, (128, pairs)).T
    pb[...] = jnp.broadcast_to(pe[...], (128, rows)).T

    def relayout(q):
        amp_copy(q).wait()
        steps = part_rows // 512

        @pl.loop(0, steps, unroll=2)
        def _(i):
            base = pl.multiple_of(q * part_rows + i * 512, 512)
            ab = jnp.concatenate([xbuf[pl.ds(base, 256), :], xbuf[pl.ds(base + 256, 256), :]], axis=1)
            res = jnp.dot(perm[...], ab, preferred_element_type=F32)
            for b in range(2):
                p0 = pl.multiple_of((q * part_rows) // 16 + i * 32 + b * 16, 16)
                for t in range(2):
                    m = mb[t, pl.ds(p0, 16), :]
                    for kt in range(8):
                        o = t * 128 + kt * 16
                        lhs[pl.ds(p0, 16), pl.ds(t * kdim + kt * 128, 128)] = (
                            res[o:o + 16, b * 128:b * 128 + 128] * m).astype(BF16)

    relayout(0)
    pl.semaphore_wait(barrier, len(friends))

    def gsl(g):
        return pl.ds(GROUPS[g][0], GROUPS[g][1])

    def first_x(g, d):
        return remote(vt.at[gsl(g), 0], vb.at[gsl(g), 0, x, z, k], es.at[g, d], er.at[g, d, k], dev(d, 0, 0))

    def first_z(g, d):
        return remote(vt.at[gsl(g), 1], vb.at[gsl(g), 1, x, z, k], es.at[g, 4 + d], er.at[g, d, k], dev(0, d, 1))

    def first_zd(g):
        return (4, 3, 5, 2, 6, 1, 7) if GROUPS[g][2] else (1, 7)

    def first_partner(g):
        return remote(vt.at[gsl(g), 1 - k], vb.at[gsl(g), 1 - k, x, z, k], es.at[g, 0], er.at[g, 0, k], partner)

    def fsl(f):
        return pl.ds(FIRST[f][0], FIRST[f][1])

    def p_first(f, d, t):
        return remote(vt.at[fsl(f), t], vb.at[fsl(f), t, x, z, k], fs.at[f, d, t], fr.at[f, d, k], dev(0, d, t))

    def p_partner_first(f):
        return remote(vt.at[fsl(f), 1 - k], vb.at[fsl(f), 1 - k, x, z, k], fs.at[f, 0, 0], fr.at[f, 0, k], partner)

    def p_first_wait(f):
        def got(d, kk):
            remote(vt.at[fsl(f), 0], vb.at[fsl(f), k, x, za(-d), kk], fs.at[f, d, 0], fr.at[f, d, kk], partner).wait_recv()

        for d in range(1, ZN):
            for kk in range(KN):
                got(d, kk)
        got(0, 1 - k)

    def p_col(c, dx, zs=slice(None)):
        return vb.at[c, k, xa(dx), zs]

    def p_x(c, n):
        if n < 2:
            return same(p_col(c, 0), cs.at[c, n], cr.at[c, n], dev((1, XN - 1)[n], 0, k))
        if n == 2:
            return same(p_col(c, -1, slice(0, ZN // 2)), cs.at[c, 2], cr.at[c, 2], dev(1, 0, k))
        return same(p_col(c, 1, slice(ZN // 2, ZN)), cs.at[c, 3], cr.at[c, 3], dev(XN - 1, 0, k))

    def p_partner(c, dx):
        return same(p_col(c, dx), ks.at[c, dx % XN], kr.at[c, dx % XN], partner)

    def p_stage(c, st):
        if st == 0:
            for f, (c0, _) in enumerate(FIRST):
                if c == c0:
                    p_first_wait(f)
            p_x(c, 0).start()
            p_x(c, 1).start()
            p_partner(c, 0).start()
        elif st == 1:
            for n, dx in ((0, -1), (1, 1)):
                p_x(c, n).wait_recv()
                p_x(c, n + 2).start()
                p_partner(c, dx).start()
        elif st == 2:
            p_x(c, 2).wait_recv()
            p_x(c, 3).wait_recv()
            p_partner(c, 2).start()
        else:
            for d in range(XN):
                p_partner(c, d).wait_recv()

    def start_p(f):
        for d in (4, 3, 5, 2, 6, 1, 7):
            for t in range(2):
                p_first(f, d, t).start()
        p_partner_first(f).start()

    start_p(0)
    for g in range(NG):
        for d in first_zd(g):
            first_z(g, d).start()
        for d in (2, 1, 3):
            first_x(g, d).start()
        first_partner(g).start()
    for f in range(1, len(FIRST)):
        start_p(f)

    def first_wait(g, ds):
        for d in ds:
            for kk in range(KN):
                remote(vt.at[gsl(g), 0], vb.at[gsl(g), 0, x, z, kk], es.at[g, d], er.at[g, d, kk], partner).wait_recv()
        remote(vt.at[gsl(g), 0], vb.at[gsl(g), 0, x, z, 0], es.at[g, 0], er.at[g, 0, 1 - k], partner).wait_recv()

    def row(g, dz, xs=slice(None)):
        return vb.at[gsl(g), 0, xs, za(dz)]

    def row_direct(g, d):
        return same(row(g, 0), qs.at[g, d], qr.at[g, d], dev(0, d, 0))

    def row_step(g, n, way):
        far = n == 3
        if way == 0:
            ref = row(g, -n, slice(0, XN // 2) if far else slice(None))
            return same(ref, qs.at[g, 2 * n], qr.at[g, 2 * n], dev(0, 1, 0))
        ref = row(g, n, slice(XN // 2, XN) if far else slice(None))
        return same(ref, qs.at[g, 2 * n + 1], qr.at[g, 2 * n + 1], dev(0, ZN - 1, 0))

    def row_partner(g, dz):
        return same(row(g, dz), ps.at[g, dz % ZN], pr.at[g, dz % ZN], partner)

    def ring_step(g, n, way):
        if way == 0:
            ref = vb.at[gsl(g), 1, x, za(-n)]
            return same(ref, qs.at[g, 2 * n - 2], qr.at[g, 2 * n - 2], dev(0, 1, 1))
        ref = vb.at[gsl(g), 1, x, za(n)]
        return same(ref, qs.at[g, 2 * n - 1], qr.at[g, 2 * n - 1], dev(0, ZN - 1, 1))

    def col(g, dx, zs=slice(None)):
        return vb.at[gsl(g), 1, xa(dx), zs]

    def col_direct(g, d):
        return same(col(g, 0), qs.at[g, 5 + d], qr.at[g, 5 + d], dev(d, 0, 1))

    def col_forward(g, way):
        if way == 0:
            return same(col(g, -1, slice(0, ZN // 2)), qs.at[g, 9], qr.at[g, 9], dev(1, 0, 1))
        return same(col(g, 1, slice(ZN // 2, ZN)), qs.at[g, 10], qr.at[g, 10], dev(XN - 1, 0, 1))

    def col_partner(g, dx):
        return same(col(g, dx), ps.at[g, dx % XN], pr.at[g, dx % XN], partner)

    def rows_all(g):
        if GROUPS[g][2]:
            return [row_direct(g, d) for d in (4, 3, 5, 2, 6, 1, 7)]
        return [row_step(g, n, w) for n in range(4) for w in range(2)]

    def cols_all(g):
        if GROUPS[g][2]:
            return [col_direct(g, d) for d in (2, 1, 3)]
        out = [ring_step(g, n, w) for n in (1, 2) for w in range(2)] + [ring_step(g, 3, 0)]
        return out + [col_direct(g, 1), col_direct(g, 3), col_forward(g, 0), col_forward(g, 1)]

    def stage_rows(g, st):
        direct = GROUPS[g][2]
        if st == 0:
            first_wait(g, (1, 2, 3))
            for cp in rows_all(g) if direct else (row_step(g, 0, 0), row_step(g, 0, 1)):
                cp.start()
            row_partner(g, 0).start()
        elif direct and st == 1:
            for d in (1, 7, 2, 6, 3, 5, 4):
                row_direct(g, d).wait_recv()
                row_partner(g, -d).start()
        elif not direct and st <= 3:
            row_step(g, st - 1, 0).wait_recv()
            row_step(g, st, 0).start()
            row_partner(g, -st).start()
            row_step(g, st - 1, 1).wait_recv()
            row_step(g, st, 1).start()
            row_partner(g, st).start()
        elif not direct and st == 4:
            row_step(g, 3, 0).wait_recv()
            row_step(g, 3, 1).wait_recv()
            row_partner(g, 4).start()
        elif st == (2 if direct else 6):
            for d in range(XN):
                col_partner(g, d).wait_recv()

    def stage_cols(g, st):
        direct = GROUPS[g][2]
        if st == 0:
            first_wait(g, range(1, ZN) if direct else (1, 7))
        if not direct and st <= 2:
            if st:
                ring_step(g, st, 0).wait_recv()
            ring_step(g, st + 1, 0).start()
            if st:
                ring_step(g, st, 1).wait_recv()
            if st < 2:
                ring_step(g, st + 1, 1).start()
        elif st == (0 if direct else 3):
            if not direct:
                ring_step(g, 3, 0).wait_recv()
            for d in (2, 1, 3) if direct else (1, 3):
                col_direct(g, d).start()
            col_partner(g, 0).start()
        elif direct and st == 1:
            for d in (1, 3, 2):
                col_direct(g, d).wait_recv()
                col_partner(g, -d).start()
        elif not direct and st == 4:
            col_direct(g, 1).wait_recv()
            col_forward(g, 0).start()
            col_partner(g, -1).start()
            col_direct(g, 3).wait_recv()
            col_forward(g, 1).start()
            col_partner(g, 1).start()
        elif not direct and st == 5:
            col_forward(g, 0).wait_recv()
            col_forward(g, 1).wait_recv()
            col_partner(g, 2).start()
        elif st == (2 if direct else 6):
            for d in range(ZN):
                row_partner(g, d).wait_recv()

    def stages(steps):
        for kind, n, st in steps:
            if kind == "P":
                p_stage(n, st)
            else:
                @pl.when(k == 0)
                def _():
                    stage_rows(n, st)

                @pl.when(k == 1)
                def _():
                    stage_cols(n, st)

    def ycopy(b, n):
        c = pl.ds(*BLOCKS[b])
        lo, hi = pl.ds(0, half), pl.ds(half, half)
        src, dst, to = (
            (snd2.at[c, lo], r2a.at[c], jm),
            (snd2.at[c, hi], r2b.at[c], jp),
            (s_p.at[c, lo], r_m.at[c, lo], jp),
            (s_m.at[c, hi], r_p.at[c, hi], jm),
            (s_p.at[c, hi], r_m.at[c, hi], jp),
            (s_m.at[c, lo], r_p.at[c, lo], jm),
        )[n]
        return remote(src, dst, ys.at[b, n], yr.at[b, n], ydev(to))

    def compute(b, slots):
        c0, n = BLOCKS[b]

        def part(d):
            sl = pl.ds(pl.multiple_of(d * rows, rows), rows)
            total = None
            for t in range(2):
                rhs = [vb[c, t].reshape(kdim, W) for c in range(c0, c0 + n)]
                rhs = rhs[0] if n == 1 else jnp.concatenate(rhs, axis=1)
                term = jnp.dot(lhs[sl, t * kdim:(t + 1) * kdim], rhs, preferred_element_type=F32)
                total = term if total is None else total + term
            return [total[:, i * W:(i + 1) * W] for i in range(n)]

        stages(slots[0])
        for i, res in enumerate(part(jo)):
            snd2[c0 + i] = res.astype(BF16)
        ycopy(b, 0).start()
        ycopy(b, 1).start()
        stages(slots[1])
        for i, res in enumerate(part(jp)):
            s_p[c0 + i, 0:half] = res[0:half].astype(BF16)
            h_p[c0 + i] = res[half:]
        ycopy(b, 2).start()
        stages(slots[2])
        for i, res in enumerate(part(jm)):
            s_m[c0 + i, half:rows] = res[half:].astype(BF16)
            h_m[c0 + i] = res[0:half]
        ycopy(b, 3).start()
        stages(slots[3])
        for i, res in enumerate(part(j)):
            own[c0 + i] = res

    def block_chunks(b):
        c0, n = BLOCKS[b]
        return range(c0, c0 + n)

    def combine(b):
        ycopy(b, 1).wait_recv()
        for c in block_chunks(b):
            s_p[c, half:rows] = (h_p[c] + r2b[c].astype(F32)).astype(BF16)
        ycopy(b, 4).start()
        ycopy(b, 0).wait_recv()
        for c in block_chunks(b):
            s_m[c, 0:half] = (h_m[c] + r2a[c].astype(F32)).astype(BF16)
        ycopy(b, 5).start()

    def final(b):
        for n in (2, 3, 4, 5):
            ycopy(b, n).wait_recv()
        for c in block_chunks(b):
            cols = slice(c * W, (c + 1) * W)
            total = own[c] + r_p[c].astype(F32) + r_m[c].astype(F32)
            out[:, cols] = (total / (ve[:, cols] - pb[...])).astype(BF16)

    own_copy.wait()
    stages(PRE[0])
    for q in range(1, parts):
        relayout(q)
        stages(PRE[q])

    for b in range(NB):
        compute(b, PLAN[b])
        if b >= LAG:
            combine(b - LAG)
        if b >= LAG2:
            final(b - LAG2)
    for b in range(NB - LAG, NB):
        combine(b)
    for b in range(NB - LAG2, NB):
        final(b)

    for g in range(NG):
        for d in first_zd(g):
            first_z(g, d).wait_send()
        for d in (1, 2, 3):
            first_x(g, d).wait_send()
        first_partner(g).wait_send()
    for f in range(len(FIRST)):
        for d in range(1, ZN):
            for t in range(2):
                p_first(f, d, t).wait_send()
        p_partner_first(f).wait_send()

    @pl.loop(0, NP)
    def _(c):
        for n in range(4):
            p_x(c, n).wait_send()
            p_partner(c, n).wait_send()

    @pl.when(k == 0)
    def _():
        for g in range(NG):
            for cp in rows_all(g) + [row_partner(g, d) for d in range(ZN)]:
                cp.wait_send()

    @pl.when(k == 1)
    def _():
        for g in range(NG):
            for cp in cols_all(g) + [col_partner(g, d) for d in range(XN)]:
                cp.wait_send()

    for b in range(NB):
        for n in range(6):
            ycopy(b, n).wait_send()


def on_device(amplitudes, tile_mask, integrals, pair_energy, virt_energy):
    pairs, tiles, kdim = amplitudes.shape
    depth, ab = integrals.shape[1:]
    rows = pairs // YN
    half = rows // 2
    chunks = ab // W
    kt = kdim // 128
    amp = amplitudes.reshape(pairs, tiles, kt, 128).transpose(0, 2, 1, 3).reshape(pairs * kt * tiles, 128)
    vmem = pl.BlockSpec(memory_space=pltpu.VMEM)
    dma = pltpu.SemaphoreType.DMA
    return pl.pallas_call(
        kernel,
        out_shape=pltpu.VMEM((rows, ab), BF16),
        in_specs=[pl.BlockSpec(memory_space=pltpu.HBM)] * 5,
        out_specs=vmem,
        scratch_shapes=[
            pltpu.VMEM((tiles, pairs), jnp.int32),
            pltpu.VMEM((1, rows), F32),
            pltpu.VMEM((1, ab), F32),
            pltpu.VMEM(amp.shape, BF16),
            pltpu.VMEM((pairs, tiles * kdim), BF16),
            pltpu.VMEM((chunks, tiles, depth, W), BF16),
            pltpu.VMEM((chunks, tiles, XN, ZN, KN, depth, W), BF16),
            pltpu.VMEM((256, 256), BF16),
            pltpu.VMEM((tiles, pairs, 128), F32),
            pltpu.VMEM((rows, 128), F32),
            pltpu.VMEM((chunks, rows, W), BF16),
            pltpu.VMEM((chunks, rows, W), BF16),
            pltpu.VMEM((chunks, rows, W), BF16),
            pltpu.VMEM((chunks, half, W), BF16),
            pltpu.VMEM((chunks, half, W), BF16),
            pltpu.VMEM((chunks, rows, W), BF16),
            pltpu.VMEM((chunks, rows, W), BF16),
            pltpu.VMEM((chunks, half, W), F32),
            pltpu.VMEM((chunks, half, W), F32),
            pltpu.VMEM((chunks, rows, W), F32),
            dma((4,)),
            dma((chunks,)),
            dma((3,)),
            dma,
            dma((len(FIRST), ZN, KN)),
            dma((len(FIRST), ZN, KN)),
            dma((NP, 4)),
            dma((NP, 4)),
            dma((NP, 4)),
            dma((NP, 4)),
            dma((NG, 12)),
            dma((NG, ZN, KN)),
            dma((NG, 11)),
            dma((NG, 11)),
            dma((NG, ZN)),
            dma((NG, ZN)),
            dma((NB, 6)),
            dma((NB, 6)),
        ],
        compiler_params=pltpu.CompilerParams(collective_id=0, has_side_effects=True),
        name="ladder",
    )(amp, tile_mask.T, integrals, pair_energy[None, :], virt_energy[None, :])


def solution(mesh):
    placed = (
        P("pair", "virt", None),
        P("pair", "virt"),
        P("virt", "pair", None),
        P(("pair", "virt")),
        P(),
    )
    return jax.shard_map(
        on_device, mesh=mesh, in_specs=placed, out_specs=P(("pair", "virt"), None), check_vma=False
    )
```

```python
import functools

import jax
import jax.numpy as jnp
from jax import lax
from jax.experimental import pallas as pl
from jax.experimental.pallas import tpu as pltpu
from jax.sharding import PartitionSpec as P

MESH = pl.DeviceIdType.MESH
XN, ZN, KN, YN = 4, 8, 2, 4
W = 128
F32, BF16 = jnp.float32, jnp.bfloat16
NP = 3
FIRST = ((0, 1), (1, 2))
GROUPS = ((3, 2, False), (5, 3, False))
NG = len(GROUPS)
PRE = (
    (),
    (),
    (),
    (('Q', 0, 0), ('Q', 1, 0), ('P', 0, 0), ('P', 1, 0), ('P', 2, 0), ('Q', 0, 1), ('P', 0, 1), ('Q', 1, 1), ('P', 1, 1), ('P', 0, 2), ('Q', 0, 2), ('Q', 1, 2), ('P', 2, 1)),
)
BLOCKS = ((0, 1), (1, 1), (2, 1), (3, 2), (5, 2), (7, 1))
PLAN = (
    ((('P', 0, 3),), (('P', 1, 2),), (), (('Q', 0, 3),)),
    ((('Q', 1, 3), ('P', 1, 3)), (('P', 2, 2),), (), ()),
    ((('P', 2, 3),), (('Q', 0, 4), ('Q', 1, 4)), (), ()),
    ((('Q', 0, 5), ('Q', 0, 6)), (), (), (('Q', 1, 5),)),
    ((('Q', 1, 6),), (), (), ()),
    ((), (), (), ()),
)
NB = len(BLOCKS)
LAG, LAG2 = 1, 3


def kernel(amp, mask_in, vin, pe_in, ve_in, out, mask, pe, ve, xbuf, lhs, vt, vb, perm, mb, pb, snd2, s_p, s_m,
           r2a, r2b, r_p, r_m, h_p, h_m, own, asem, tsem, isem, vsem,
           fs, fr, cs, cr, ks, kr, es, er, qs, qr, ps, pr, ys, yr):
    pairs = lhs.shape[0]
    rows = pairs // YN
    half = rows // 2
    chunks, _, depth, _ = vt.shape
    kdim = XN * ZN * KN * depth

    me = lax.axis_index("pair")
    j = lax.axis_index("virt")
    k = me % KN
    z = (me // KN) % ZN
    x = me // (KN * ZN)

    def dev(dx, dz, kk):
        return {"pair": (((x + dx) % XN) * ZN + (z + dz) % ZN) * KN + kk, "virt": j}

    def ydev(jj):
        return {"pair": me, "virt": jj}

    def xa(d):
        return (x + d + XN) % XN

    def za(d):
        return (z + d + ZN) % ZN

    jp, jm, jo = (j + 1) % YN, (j + YN - 1) % YN, (j + 2) % YN
    partner = dev(0, 0, 1 - k)

    def remote(src, dst, ss, rs, to):
        return pltpu.make_async_remote_copy(
            src_ref=src, dst_ref=dst, send_sem=ss, recv_sem=rs, device_id=to, device_id_type=MESH)

    def same(ref, ss, rs, to):
        return remote(ref, ref, ss, rs, to)

    parts = asem.shape[0]
    part_rows = amp.shape[0] // parts

    def amp_copy(q):
        sl = pl.ds(q * part_rows, part_rows)
        return pltpu.make_async_copy(amp.at[sl], xbuf.at[sl], asem.at[q])

    def tile_copy(c):
        return pltpu.make_async_copy(vin.at[:, :, c * W:(c + 1) * W], vt.at[c], tsem.at[c])

    barrier = pltpu.get_barrier_semaphore()
    friends = [dev(d, 0, kk) for d in range(1, XN) for kk in range(KN)]
    friends += [dev(0, d, kk) for d in range(1, ZN) for kk in range(KN)]
    friends += [partner, ydev(jp), ydev(jm)]
    for to in friends:
        pl.semaphore_signal(barrier, inc=1, device_id=to, device_id_type=MESH)

    for c in range(chunks):
        tile_copy(c).start()
    for q in range(parts):
        amp_copy(q).start()
    small = [pltpu.make_async_copy(src, dst, isem.at[i])
             for i, (src, dst) in enumerate(((mask_in, mask), (pe_in, pe), (ve_in, ve)))]
    for cp in small:
        cp.start()
    for c in range(chunks):
        tile_copy(c).wait()
    own_copy = pltpu.make_async_copy(vt.at[:, k], vb.at[:, k, x, z, k], vsem)
    own_copy.start()

    def relayout(q):
        amp_copy(q).wait()
        steps = part_rows // 512

        @pl.loop(0, steps, unroll=2)
        def _(i):
            base = pl.multiple_of(q * part_rows + i * 512, 512)
            ab = jnp.concatenate([xbuf[pl.ds(base, 256), :], xbuf[pl.ds(base + 256, 256), :]], axis=1)
            res = jnp.dot(perm[...], ab, preferred_element_type=F32)
            for b in range(2):
                p0 = pl.multiple_of((q * part_rows) // 16 + i * 32 + b * 16, 16)
                for t in range(2):
                    m = mb[t, pl.ds(p0, 16), :]
                    for kt in range(8):
                        o = t * 128 + kt * 16
                        lhs[pl.ds(p0, 16), pl.ds(t * kdim + kt * 128, 128)] = (
                            res[o:o + 16, b * 128:b * 128 + 128] * m).astype(BF16)

    pl.semaphore_wait(barrier, len(friends))

    def gsl(g):
        return pl.ds(GROUPS[g][0], GROUPS[g][1])

    def first_x(g, d):
        return remote(vt.at[gsl(g), 0], vb.at[gsl(g), 0, x, z, k], es.at[g, d], er.at[g, d, k], dev(d, 0, 0))

    def first_z(g, d):
        return remote(vt.at[gsl(g), 1], vb.at[gsl(g), 1, x, z, k], es.at[g, 4 + d], er.at[g, d, k], dev(0, d, 1))

    def first_zd(g):
        return (4, 3, 5, 2, 6, 1, 7) if GROUPS[g][2] else (1, 7)

    def first_partner(g):
        return remote(vt.at[gsl(g), 1 - k], vb.at[gsl(g), 1 - k, x, z, k], es.at[g, 0], er.at[g, 0, k], partner)

    def fsl(f):
        return pl.ds(FIRST[f][0], FIRST[f][1])

    def p_first(f, d, t):
        return remote(vt.at[fsl(f), t], vb.at[fsl(f), t, x, z, k], fs.at[f, d, t], fr.at[f, d, k], dev(0, d, t))

    def p_partner_first(f):
        return remote(vt.at[fsl(f), 1 - k], vb.at[fsl(f), 1 - k, x, z, k], fs.at[f, 0, 0], fr.at[f, 0, k], partner)

    def p_first_wait(f):
        def got(d, kk):
            remote(vt.at[fsl(f), 0], vb.at[fsl(f), k, x, za(-d), kk], fs.at[f, d, 0], fr.at[f, d, kk], partner).wait_recv()

        for d in range(1, ZN):
            for kk in range(KN):
                got(d, kk)
        got(0, 1 - k)

    def p_col(c, dx, zs=slice(None)):
        return vb.at[c, k, xa(dx), zs]

    def p_x(c, n):
        if n < 2:
            return same(p_col(c, 0), cs.at[c, n], cr.at[c, n], dev((1, XN - 1)[n], 0, k))
        if n == 2:
            return same(p_col(c, -1, slice(0, ZN // 2)), cs.at[c, 2], cr.at[c, 2], dev(1, 0, k))
        return same(p_col(c, 1, slice(ZN // 2, ZN)), cs.at[c, 3], cr.at[c, 3], dev(XN - 1, 0, k))

    def p_partner(c, dx):
        return same(p_col(c, dx), ks.at[c, dx % XN], kr.at[c, dx % XN], partner)

    def p_stage(c, st):
        if st == 0:
            for f, (c0, _) in enumerate(FIRST):
                if c == c0:
                    p_first_wait(f)
            p_x(c, 0).start()
            p_x(c, 1).start()
            p_partner(c, 0).start()
        elif st == 1:
            for n, dx in ((0, -1), (1, 1)):
                p_x(c, n).wait_recv()
                p_x(c, n + 2).start()
                p_partner(c, dx).start()
        elif st == 2:
            p_x(c, 2).wait_recv()
            p_x(c, 3).wait_recv()
            p_partner(c, 2).start()
        else:
            for d in range(XN):
                p_partner(c, d).wait_recv()

    def start_p(f):
        for d in (4, 3, 5, 2, 6, 1, 7):
            for t in range(2):
                p_first(f, d, t).start()
        p_partner_first(f).start()

    start_p(0)
    for g in range(NG):
        for d in first_zd(g):
            first_z(g, d).start()
        for d in (2, 1, 3):
            first_x(g, d).start()
        first_partner(g).start()
    for f in range(1, len(FIRST)):
        start_p(f)

    def first_wait(g, ds):
        for d in ds:
            for kk in range(KN):
                remote(vt.at[gsl(g), 0], vb.at[gsl(g), 0, x, z, kk], es.at[g, d], er.at[g, d, kk], partner).wait_recv()
        remote(vt.at[gsl(g), 0], vb.at[gsl(g), 0, x, z, 0], es.at[g, 0], er.at[g, 0, 1 - k], partner).wait_recv()

    def row(g, dz, xs=slice(None)):
        return vb.at[gsl(g), 0, xs, za(dz)]

    def row_direct(g, d):
        return same(row(g, 0), qs.at[g, d], qr.at[g, d], dev(0, d, 0))

    def row_step(g, n, way):
        far = n == 3
        if way == 0:
            ref = row(g, -n, slice(0, XN // 2) if far else slice(None))
            return same(ref, qs.at[g, 2 * n], qr.at[g, 2 * n], dev(0, 1, 0))
        ref = row(g, n, slice(XN // 2, XN) if far else slice(None))
        return same(ref, qs.at[g, 2 * n + 1], qr.at[g, 2 * n + 1], dev(0, ZN - 1, 0))

    def row_partner(g, dz):
        return same(row(g, dz), ps.at[g, dz % ZN], pr.at[g, dz % ZN], partner)

    def ring_step(g, n, way):
        if way == 0:
            ref = vb.at[gsl(g), 1, x, za(-n)]
            return same(ref, qs.at[g, 2 * n - 2], qr.at[g, 2 * n - 2], dev(0, 1, 1))
        ref = vb.at[gsl(g), 1, x, za(n)]
        return same(ref, qs.at[g, 2 * n - 1], qr.at[g, 2 * n - 1], dev(0, ZN - 1, 1))

    def col(g, dx, zs=slice(None)):
        return vb.at[gsl(g), 1, xa(dx), zs]

    def col_direct(g, d):
        return same(col(g, 0), qs.at[g, 5 + d], qr.at[g, 5 + d], dev(d, 0, 1))

    def col_forward(g, way):
        if way == 0:
            return same(col(g, -1, slice(0, ZN // 2)), qs.at[g, 9], qr.at[g, 9], dev(1, 0, 1))
        return same(col(g, 1, slice(ZN // 2, ZN)), qs.at[g, 10], qr.at[g, 10], dev(XN - 1, 0, 1))

    def col_partner(g, dx):
        return same(col(g, dx), ps.at[g, dx % XN], pr.at[g, dx % XN], partner)

    def rows_all(g):
        if GROUPS[g][2]:
            return [row_direct(g, d) for d in (4, 3, 5, 2, 6, 1, 7)]
        return [row_step(g, n, w) for n in range(4) for w in range(2)]

    def cols_all(g):
        if GROUPS[g][2]:
            return [col_direct(g, d) for d in (2, 1, 3)]
        out = [ring_step(g, n, w) for n in (1, 2) for w in range(2)] + [ring_step(g, 3, 0)]
        return out + [col_direct(g, 1), col_direct(g, 3), col_forward(g, 0), col_forward(g, 1)]

    def stage_rows(g, st):
        direct = GROUPS[g][2]
        if st == 0:
            first_wait(g, (1, 2, 3))
            for cp in rows_all(g) if direct else (row_step(g, 0, 0), row_step(g, 0, 1)):
                cp.start()
            row_partner(g, 0).start()
        elif direct and st == 1:
            for d in (1, 7, 2, 6, 3, 5, 4):
                row_direct(g, d).wait_recv()
                row_partner(g, -d).start()
        elif not direct and st <= 3:
            row_step(g, st - 1, 0).wait_recv()
            row_step(g, st, 0).start()
            row_partner(g, -st).start()
            row_step(g, st - 1, 1).wait_recv()
            row_step(g, st, 1).start()
            row_partner(g, st).start()
        elif not direct and st == 4:
            row_step(g, 3, 0).wait_recv()
            row_step(g, 3, 1).wait_recv()
            row_partner(g, 4).start()
        elif st == (2 if direct else 6):
            for d in range(XN):
                col_partner(g, d).wait_recv()

    def stage_cols(g, st):
        direct = GROUPS[g][2]
        if st == 0:
            first_wait(g, range(1, ZN) if direct else (1, 7))
        if not direct and st <= 2:
            if st:
                ring_step(g, st, 0).wait_recv()
            ring_step(g, st + 1, 0).start()
            if st:
                ring_step(g, st, 1).wait_recv()
            if st < 2:
                ring_step(g, st + 1, 1).start()
        elif st == (0 if direct else 3):
            if not direct:
                ring_step(g, 3, 0).wait_recv()
            for d in (2, 1, 3) if direct else (1, 3):
                col_direct(g, d).start()
            col_partner(g, 0).start()
        elif direct and st == 1:
            for d in (1, 3, 2):
                col_direct(g, d).wait_recv()
                col_partner(g, -d).start()
        elif not direct and st == 4:
            col_direct(g, 1).wait_recv()
            col_forward(g, 0).start()
            col_partner(g, -1).start()
            col_direct(g, 3).wait_recv()
            col_forward(g, 1).start()
            col_partner(g, 1).start()
        elif not direct and st == 5:
            col_forward(g, 0).wait_recv()
            col_forward(g, 1).wait_recv()
            col_partner(g, 2).start()
        elif st == (2 if direct else 6):
            for d in range(ZN):
                row_partner(g, d).wait_recv()

    def stages(steps):
        for kind, n, st in steps:
            if kind == "P":
                p_stage(n, st)
            else:
                @pl.when(k == 0)
                def _():
                    stage_rows(n, st)

                @pl.when(k == 1)
                def _():
                    stage_cols(n, st)

    def ycopy(b, n):
        c = pl.ds(*BLOCKS[b])
        lo, hi = pl.ds(0, half), pl.ds(half, half)
        src, dst, to = (
            (snd2.at[c, lo], r2a.at[c], jm),
            (snd2.at[c, hi], r2b.at[c], jp),
            (s_p.at[c, lo], r_m.at[c, lo], jp),
            (s_m.at[c, hi], r_p.at[c, hi], jm),
            (s_p.at[c, hi], r_m.at[c, hi], jp),
            (s_m.at[c, lo], r_p.at[c, lo], jm),
        )[n]
        return remote(src, dst, ys.at[b, n], yr.at[b, n], ydev(to))

    def compute(b, slots):
        c0, n = BLOCKS[b]

        def part(d):
            sl = pl.ds(pl.multiple_of(d * rows, rows), rows)
            total = None
            for t in range(2):
                rhs = [vb[c, t].reshape(kdim, W) for c in range(c0, c0 + n)]
                rhs = rhs[0] if n == 1 else jnp.concatenate(rhs, axis=1)
                term = jnp.dot(lhs[sl, t * kdim:(t + 1) * kdim], rhs, preferred_element_type=F32)
                total = term if total is None else total + term
            return [total[:, i * W:(i + 1) * W] for i in range(n)]

        stages(slots[0])
        for i, res in enumerate(part(jo)):
            snd2[c0 + i] = res.astype(BF16)
        ycopy(b, 0).start()
        ycopy(b, 1).start()
        stages(slots[1])
        for i, res in enumerate(part(jp)):
            s_p[c0 + i, 0:half] = res[0:half].astype(BF16)
            h_p[c0 + i] = res[half:]
        ycopy(b, 2).start()
        stages(slots[2])
        for i, res in enumerate(part(jm)):
            s_m[c0 + i, half:rows] = res[half:].astype(BF16)
            h_m[c0 + i] = res[0:half]
        ycopy(b, 3).start()
        stages(slots[3])
        for i, res in enumerate(part(j)):
            own[c0 + i] = res

    def block_chunks(b):
        c0, n = BLOCKS[b]
        return range(c0, c0 + n)

    def combine(b):
        ycopy(b, 1).wait_recv()
        for c in block_chunks(b):
            s_p[c, half:rows] = (h_p[c] + r2b[c].astype(F32)).astype(BF16)
        ycopy(b, 4).start()
        ycopy(b, 0).wait_recv()
        for c in block_chunks(b):
            s_m[c, 0:half] = (h_m[c] + r2a[c].astype(F32)).astype(BF16)
        ycopy(b, 5).start()

    def final(b):
        for n in (2, 3, 4, 5):
            ycopy(b, n).wait_recv()
        for c in block_chunks(b):
            cols = slice(c * W, (c + 1) * W)
            total = own[c] + r_p[c].astype(F32) + r_m[c].astype(F32)
            out[:, cols] = (total / (ve[:, cols] - pb[...])).astype(BF16)

    r = lax.broadcasted_iota(jnp.int32, (256, 256), 0)
    s = lax.broadcasted_iota(jnp.int32, (256, 256), 1)
    target = (r & 15) * 16 + ((r >> 4) & 7) * 2 + (r >> 7)
    perm[...] = jnp.where(s == target, 1.0, 0.0).astype(BF16)
    for cp in small:
        cp.wait()
    for t in range(2):
        line = mask[t:t + 1, :].astype(F32)
        mb[t] = jnp.broadcast_to(line, (128, pairs)).T
    pb[...] = jnp.broadcast_to(pe[...], (128, rows)).T

    own_copy.wait()
    for q in range(parts):
        relayout(q)
        stages(PRE[q])

    for b in range(NB):
        compute(b, PLAN[b])
        if b >= LAG:
            combine(b - LAG)
        if b >= LAG2:
            final(b - LAG2)
    for b in range(NB - LAG, NB):
        combine(b)
    for b in range(NB - LAG2, NB):
        final(b)

    for g in range(NG):
        for d in first_zd(g):
            first_z(g, d).wait_send()
        for d in (1, 2, 3):
            first_x(g, d).wait_send()
        first_partner(g).wait_send()
    for f in range(len(FIRST)):
        for d in range(1, ZN):
            for t in range(2):
                p_first(f, d, t).wait_send()
        p_partner_first(f).wait_send()

    @pl.loop(0, NP)
    def _(c):
        for n in range(4):
            p_x(c, n).wait_send()
            p_partner(c, n).wait_send()

    @pl.when(k == 0)
    def _():
        for g in range(NG):
            for cp in rows_all(g) + [row_partner(g, d) for d in range(ZN)]:
                cp.wait_send()

    @pl.when(k == 1)
    def _():
        for g in range(NG):
            for cp in cols_all(g) + [col_partner(g, d) for d in range(XN)]:
                cp.wait_send()

    for b in range(NB):
        for n in range(6):
            ycopy(b, n).wait_send()


def on_device(amplitudes, tile_mask, integrals, pair_energy, virt_energy):
    pairs, tiles, kdim = amplitudes.shape
    depth, ab = integrals.shape[1:]
    rows = pairs // YN
    half = rows // 2
    chunks = ab // W
    kt = kdim // 128
    amp = amplitudes.reshape(pairs, tiles, kt, 128).transpose(0, 2, 1, 3).reshape(pairs * kt * tiles, 128)
    vmem = pl.BlockSpec(memory_space=pltpu.VMEM)
    dma = pltpu.SemaphoreType.DMA
    return pl.pallas_call(
        kernel,
        out_shape=pltpu.VMEM((rows, ab), BF16),
        in_specs=[pl.BlockSpec(memory_space=pltpu.HBM)] * 5,
        out_specs=vmem,
        scratch_shapes=[
            pltpu.VMEM((tiles, pairs), jnp.int32),
            pltpu.VMEM((1, rows), F32),
            pltpu.VMEM((1, ab), F32),
            pltpu.VMEM(amp.shape, BF16),
            pltpu.VMEM((pairs, tiles * kdim), BF16),
            pltpu.VMEM((chunks, tiles, depth, W), BF16),
            pltpu.VMEM((chunks, tiles, XN, ZN, KN, depth, W), BF16),
            pltpu.VMEM((256, 256), BF16),
            pltpu.VMEM((tiles, pairs, 128), F32),
            pltpu.VMEM((rows, 128), F32),
            pltpu.VMEM((chunks, rows, W), BF16),
            pltpu.VMEM((chunks, rows, W), BF16),
            pltpu.VMEM((chunks, rows, W), BF16),
            pltpu.VMEM((chunks, half, W), BF16),
            pltpu.VMEM((chunks, half, W), BF16),
            pltpu.VMEM((chunks, rows, W), BF16),
            pltpu.VMEM((chunks, rows, W), BF16),
            pltpu.VMEM((chunks, half, W), F32),
            pltpu.VMEM((chunks, half, W), F32),
            pltpu.VMEM((chunks, rows, W), F32),
            dma((4,)),
            dma((chunks,)),
            dma((3,)),
            dma,
            dma((len(FIRST), ZN, KN)),
            dma((len(FIRST), ZN, KN)),
            dma((NP, 4)),
            dma((NP, 4)),
            dma((NP, 4)),
            dma((NP, 4)),
            dma((NG, 12)),
            dma((NG, ZN, KN)),
            dma((NG, 11)),
            dma((NG, 11)),
            dma((NG, ZN)),
            dma((NG, ZN)),
            dma((NB, 6)),
            dma((NB, 6)),
        ],
        compiler_params=pltpu.CompilerParams(collective_id=0, has_side_effects=True),
        name="ladder",
    )(amp, tile_mask.T, integrals, pair_energy[None, :], virt_energy[None, :])


def solution(mesh):
    placed = (
        P("pair", "virt", None),
        P("pair", "virt"),
        P("virt", "pair", None),
        P(("pair", "virt")),
        P(),
    )
    return jax.shard_map(
        on_device, mesh=mesh, in_specs=placed, out_specs=P(("pair", "virt"), None), check_vma=False
    )
```

```python
import functools

import jax
import jax.numpy as jnp
from jax import lax
from jax.experimental import pallas as pl
from jax.experimental.pallas import tpu as pltpu
from jax.sharding import PartitionSpec as P

MESH = pl.DeviceIdType.MESH
XN, ZN, KN, YN = 4, 8, 2, 4
W = 128
F32, BF16 = jnp.float32, jnp.bfloat16
NP = 3
FIRST = ((0, 1), (1, 2))
GROUPS = ((3, 2, False), (5, 3, False))
NG = len(GROUPS)
PRE = (
    (),
    (),
    (),
    (('Q', 0, 0), ('Q', 1, 0), ('P', 0, 0), ('P', 1, 0), ('P', 2, 0), ('Q', 0, 1), ('P', 0, 1), ('Q', 1, 1), ('P', 1, 1), ('P', 0, 2), ('Q', 0, 2), ('Q', 1, 2), ('P', 2, 1)),
)
BLOCKS = ((0, 1), (1, 1), (2, 1), (3, 2), (5, 2), (7, 1))
PLAN = (
    ((('P', 0, 3),), (('P', 1, 2),), (('Q', 0, 3),), ()),
    ((('Q', 1, 3), ('P', 1, 3)), (('P', 2, 2),), (), (('Q', 0, 4),)),
    ((('P', 2, 3),), (('Q', 1, 4),), (), ()),
    ((('Q', 0, 5), ('Q', 0, 6)), (), (), (('Q', 1, 5),)),
    ((('Q', 1, 6),), (), (), ()),
    ((), (), (), ()),
)
NB = len(BLOCKS)
LAG, LAG2 = 1, 3


def kernel(amp, mask_in, vin, pe_in, ve_in, out, mask, pe, ve, xbuf, lhs, vt, vb, perm, mb, pb, snd2, s_p, s_m,
           r2a, r2b, r_p, r_m, h_p, h_m, own, asem, tsem, isem, vsem,
           fs, fr, cs, cr, ks, kr, es, er, qs, qr, ps, pr, ys, yr):
    pairs = lhs.shape[0]
    rows = pairs // YN
    half = rows // 2
    chunks, _, depth, _ = vt.shape
    kdim = XN * ZN * KN * depth

    me = lax.axis_index("pair")
    j = lax.axis_index("virt")
    k = me % KN
    z = (me // KN) % ZN
    x = me // (KN * ZN)

    def dev(dx, dz, kk):
        return {"pair": (((x + dx) % XN) * ZN + (z + dz) % ZN) * KN + kk, "virt": j}

    def ydev(jj):
        return {"pair": me, "virt": jj}

    def xa(d):
        return (x + d + XN) % XN

    def za(d):
        return (z + d + ZN) % ZN

    jp, jm, jo = (j + 1) % YN, (j + YN - 1) % YN, (j + 2) % YN
    partner = dev(0, 0, 1 - k)

    def remote(src, dst, ss, rs, to):
        return pltpu.make_async_remote_copy(
            src_ref=src, dst_ref=dst, send_sem=ss, recv_sem=rs, device_id=to, device_id_type=MESH)

    def same(ref, ss, rs, to):
        return remote(ref, ref, ss, rs, to)

    parts = asem.shape[0]
    part_rows = amp.shape[0] // parts

    def amp_copy(q):
        sl = pl.ds(q * part_rows, part_rows)
        return pltpu.make_async_copy(amp.at[sl], xbuf.at[sl], asem.at[q])

    def tile_copy(c):
        return pltpu.make_async_copy(vin.at[:, :, c * W:(c + 1) * W], vt.at[c], tsem.at[c])

    barrier = pltpu.get_barrier_semaphore()
    friends = [dev(d, 0, kk) for d in range(1, XN) for kk in range(KN)]
    friends += [dev(0, d, kk) for d in range(1, ZN) for kk in range(KN)]
    friends += [partner, ydev(jp), ydev(jm)]
    for to in friends:
        pl.semaphore_signal(barrier, inc=1, device_id=to, device_id_type=MESH)

    for c in range(chunks):
        tile_copy(c).start()
    for q in range(parts):
        amp_copy(q).start()
    small = [pltpu.make_async_copy(src, dst, isem.at[i])
             for i, (src, dst) in enumerate(((mask_in, mask), (pe_in, pe), (ve_in, ve)))]
    for cp in small:
        cp.start()
    for c in range(chunks):
        tile_copy(c).wait()
    own_copy = pltpu.make_async_copy(vt.at[:, k], vb.at[:, k, x, z, k], vsem)
    own_copy.start()

    def relayout(q):
        amp_copy(q).wait()
        steps = part_rows // 512

        @pl.loop(0, steps, unroll=2)
        def _(i):
            base = pl.multiple_of(q * part_rows + i * 512, 512)
            ab = jnp.concatenate([xbuf[pl.ds(base, 256), :], xbuf[pl.ds(base + 256, 256), :]], axis=1)
            res = jnp.dot(perm[...], ab, preferred_element_type=F32)
            for b in range(2):
                p0 = pl.multiple_of((q * part_rows) // 16 + i * 32 + b * 16, 16)
                for t in range(2):
                    m = mb[t, pl.ds(p0, 16), :]
                    for kt in range(8):
                        o = t * 128 + kt * 16
                        lhs[pl.ds(p0, 16), pl.ds(t * kdim + kt * 128, 128)] = (
                            res[o:o + 16, b * 128:b * 128 + 128] * m).astype(BF16)

    pl.semaphore_wait(barrier, len(friends))

    def gsl(g):
        return pl.ds(GROUPS[g][0], GROUPS[g][1])

    def first_x(g, d):
        return remote(vt.at[gsl(g), 0], vb.at[gsl(g), 0, x, z, k], es.at[g, d], er.at[g, d, k], dev(d, 0, 0))

    def first_z(g, d):
        return remote(vt.at[gsl(g), 1], vb.at[gsl(g), 1, x, z, k], es.at[g, 4 + d], er.at[g, d, k], dev(0, d, 1))

    def first_zd(g):
        return (4, 3, 5, 2, 6, 1, 7) if GROUPS[g][2] else (1, 7)

    def first_partner(g):
        return remote(vt.at[gsl(g), 1 - k], vb.at[gsl(g), 1 - k, x, z, k], es.at[g, 0], er.at[g, 0, k], partner)

    def fsl(f):
        return pl.ds(FIRST[f][0], FIRST[f][1])

    def p_first(f, d, t):
        return remote(vt.at[fsl(f), t], vb.at[fsl(f), t, x, z, k], fs.at[f, d, t], fr.at[f, d, k], dev(0, d, t))

    def p_partner_first(f):
        return remote(vt.at[fsl(f), 1 - k], vb.at[fsl(f), 1 - k, x, z, k], fs.at[f, 0, 0], fr.at[f, 0, k], partner)

    def p_first_wait(f):
        def got(d, kk):
            remote(vt.at[fsl(f), 0], vb.at[fsl(f), k, x, za(-d), kk], fs.at[f, d, 0], fr.at[f, d, kk], partner).wait_recv()

        for d in range(1, ZN):
            for kk in range(KN):
                got(d, kk)
        got(0, 1 - k)

    def p_col(c, dx, zs=slice(None)):
        return vb.at[c, k, xa(dx), zs]

    def p_x(c, n):
        if n < 2:
            return same(p_col(c, 0), cs.at[c, n], cr.at[c, n], dev((1, XN - 1)[n], 0, k))
        if n == 2:
            return same(p_col(c, -1, slice(0, ZN // 2)), cs.at[c, 2], cr.at[c, 2], dev(1, 0, k))
        return same(p_col(c, 1, slice(ZN // 2, ZN)), cs.at[c, 3], cr.at[c, 3], dev(XN - 1, 0, k))

    def p_partner(c, dx):
        return same(p_col(c, dx), ks.at[c, dx % XN], kr.at[c, dx % XN], partner)

    def p_stage(c, st):
        if st == 0:
            for f, (c0, _) in enumerate(FIRST):
                if c == c0:
                    p_first_wait(f)
            p_x(c, 0).start()
            p_x(c, 1).start()
            p_partner(c, 0).start()
        elif st == 1:
            for n, dx in ((0, -1), (1, 1)):
                p_x(c, n).wait_recv()
                p_x(c, n + 2).start()
                p_partner(c, dx).start()
        elif st == 2:
            p_x(c, 2).wait_recv()
            p_x(c, 3).wait_recv()
            p_partner(c, 2).start()
        else:
            for d in range(XN):
                p_partner(c, d).wait_recv()

    def start_p(f):
        for d in (4, 3, 5, 2, 6, 1, 7):
            for t in range(2):
                p_first(f, d, t).start()
        p_partner_first(f).start()

    start_p(0)
    for g in range(NG):
        for d in first_zd(g):
            first_z(g, d).start()
        for d in (2, 1, 3):
            first_x(g, d).start()
        first_partner(g).start()
    for f in range(1, len(FIRST)):
        start_p(f)

    def first_wait(g, ds):
        for d in ds:
            for kk in range(KN):
                remote(vt.at[gsl(g), 0], vb.at[gsl(g), 0, x, z, kk], es.at[g, d], er.at[g, d, kk], partner).wait_recv()
        remote(vt.at[gsl(g), 0], vb.at[gsl(g), 0, x, z, 0], es.at[g, 0], er.at[g, 0, 1 - k], partner).wait_recv()

    def row(g, dz, xs=slice(None)):
        return vb.at[gsl(g), 0, xs, za(dz)]

    def row_direct(g, d):
        return same(row(g, 0), qs.at[g, d], qr.at[g, d], dev(0, d, 0))

    def row_step(g, n, way):
        far = n == 3
        if way == 0:
            ref = row(g, -n, slice(0, XN // 2) if far else slice(None))
            return same(ref, qs.at[g, 2 * n], qr.at[g, 2 * n], dev(0, 1, 0))
        ref = row(g, n, slice(XN // 2, XN) if far else slice(None))
        return same(ref, qs.at[g, 2 * n + 1], qr.at[g, 2 * n + 1], dev(0, ZN - 1, 0))

    def row_partner(g, dz):
        return same(row(g, dz), ps.at[g, dz % ZN], pr.at[g, dz % ZN], partner)

    def ring_step(g, n, way):
        if way == 0:
            ref = vb.at[gsl(g), 1, x, za(-n)]
            return same(ref, qs.at[g, 2 * n - 2], qr.at[g, 2 * n - 2], dev(0, 1, 1))
        ref = vb.at[gsl(g), 1, x, za(n)]
        return same(ref, qs.at[g, 2 * n - 1], qr.at[g, 2 * n - 1], dev(0, ZN - 1, 1))

    def col(g, dx, zs=slice(None)):
        return vb.at[gsl(g), 1, xa(dx), zs]

    def col_direct(g, d):
        return same(col(g, 0), qs.at[g, 5 + d], qr.at[g, 5 + d], dev(d, 0, 1))

    def col_forward(g, way):
        if way == 0:
            return same(col(g, -1, slice(0, ZN // 2)), qs.at[g, 9], qr.at[g, 9], dev(1, 0, 1))
        return same(col(g, 1, slice(ZN // 2, ZN)), qs.at[g, 10], qr.at[g, 10], dev(XN - 1, 0, 1))

    def col_partner(g, dx):
        return same(col(g, dx), ps.at[g, dx % XN], pr.at[g, dx % XN], partner)

    def rows_all(g):
        if GROUPS[g][2]:
            return [row_direct(g, d) for d in (4, 3, 5, 2, 6, 1, 7)]
        return [row_step(g, n, w) for n in range(4) for w in range(2)]

    def cols_all(g):
        if GROUPS[g][2]:
            return [col_direct(g, d) for d in (2, 1, 3)]
        out = [ring_step(g, n, w) for n in (1, 2) for w in range(2)] + [ring_step(g, 3, 0)]
        return out + [col_direct(g, 1), col_direct(g, 3), col_forward(g, 0), col_forward(g, 1)]

    def stage_rows(g, st):
        direct = GROUPS[g][2]
        if st == 0:
            first_wait(g, (1, 2, 3))
            for cp in rows_all(g) if direct else (row_step(g, 0, 0), row_step(g, 0, 1)):
                cp.start()
            row_partner(g, 0).start()
        elif direct and st == 1:
            for d in (1, 7, 2, 6, 3, 5, 4):
                row_direct(g, d).wait_recv()
                row_partner(g, -d).start()
        elif not direct and st <= 3:
            row_step(g, st - 1, 0).wait_recv()
            row_step(g, st, 0).start()
            row_partner(g, -st).start()
            row_step(g, st - 1, 1).wait_recv()
            row_step(g, st, 1).start()
            row_partner(g, st).start()
        elif not direct and st == 4:
            row_step(g, 3, 0).wait_recv()
            row_step(g, 3, 1).wait_recv()
            row_partner(g, 4).start()
        elif st == (2 if direct else 6):
            for d in range(XN):
                col_partner(g, d).wait_recv()

    def stage_cols(g, st):
        direct = GROUPS[g][2]
        if st == 0:
            first_wait(g, range(1, ZN) if direct else (1, 7))
        if not direct and st <= 2:
            if st:
                ring_step(g, st, 0).wait_recv()
            ring_step(g, st + 1, 0).start()
            if st:
                ring_step(g, st, 1).wait_recv()
            if st < 2:
                ring_step(g, st + 1, 1).start()
        elif st == (0 if direct else 3):
            if not direct:
                ring_step(g, 3, 0).wait_recv()
            for d in (2, 1, 3) if direct else (1, 3):
                col_direct(g, d).start()
            col_partner(g, 0).start()
        elif direct and st == 1:
            for d in (1, 3, 2):
                col_direct(g, d).wait_recv()
                col_partner(g, -d).start()
        elif not direct and st == 4:
            col_direct(g, 1).wait_recv()
            col_forward(g, 0).start()
            col_partner(g, -1).start()
            col_direct(g, 3).wait_recv()
            col_forward(g, 1).start()
            col_partner(g, 1).start()
        elif not direct and st == 5:
            col_forward(g, 0).wait_recv()
            col_forward(g, 1).wait_recv()
            col_partner(g, 2).start()
        elif st == (2 if direct else 6):
            for d in range(ZN):
                row_partner(g, d).wait_recv()

    def stages(steps):
        for kind, n, st in steps:
            if kind == "P":
                p_stage(n, st)
            else:
                @pl.when(k == 0)
                def _():
                    stage_rows(n, st)

                @pl.when(k == 1)
                def _():
                    stage_cols(n, st)

    def ycopy(b, n):
        c = pl.ds(*BLOCKS[b])
        lo, hi = pl.ds(0, half), pl.ds(half, half)
        src, dst, to = (
            (snd2.at[c, lo], r2a.at[c], jm),
            (snd2.at[c, hi], r2b.at[c], jp),
            (s_p.at[c, lo], r_m.at[c, lo], jp),
            (s_m.at[c, hi], r_p.at[c, hi], jm),
            (s_p.at[c, hi], r_m.at[c, hi], jp),
            (s_m.at[c, lo], r_p.at[c, lo], jm),
        )[n]
        return remote(src, dst, ys.at[b, n], yr.at[b, n], ydev(to))

    def compute(b, slots):
        c0, n = BLOCKS[b]

        def part(d):
            sl = pl.ds(pl.multiple_of(d * rows, rows), rows)
            total = None
            for t in range(2):
                rhs = [vb[c, t].reshape(kdim, W) for c in range(c0, c0 + n)]
                rhs = rhs[0] if n == 1 else jnp.concatenate(rhs, axis=1)
                term = jnp.dot(lhs[sl, t * kdim:(t + 1) * kdim], rhs, preferred_element_type=F32)
                total = term if total is None else total + term
            return [total[:, i * W:(i + 1) * W] for i in range(n)]

        stages(slots[0])
        for i, res in enumerate(part(jo)):
            snd2[c0 + i] = res.astype(BF16)
        ycopy(b, 0).start()
        ycopy(b, 1).start()
        stages(slots[1])
        for i, res in enumerate(part(jp)):
            s_p[c0 + i, 0:half] = res[0:half].astype(BF16)
            h_p[c0 + i] = res[half:]
        ycopy(b, 2).start()
        stages(slots[2])
        for i, res in enumerate(part(jm)):
            s_m[c0 + i, half:rows] = res[half:].astype(BF16)
            h_m[c0 + i] = res[0:half]
        ycopy(b, 3).start()
        stages(slots[3])
        for i, res in enumerate(part(j)):
            own[c0 + i] = res

    def block_chunks(b):
        c0, n = BLOCKS[b]
        return range(c0, c0 + n)

    def combine(b):
        ycopy(b, 1).wait_recv()
        for c in block_chunks(b):
            s_p[c, half:rows] = (h_p[c] + r2b[c].astype(F32)).astype(BF16)
        ycopy(b, 4).start()
        ycopy(b, 0).wait_recv()
        for c in block_chunks(b):
            s_m[c, 0:half] = (h_m[c] + r2a[c].astype(F32)).astype(BF16)
        ycopy(b, 5).start()

    def final(b):
        for n in (2, 3, 4, 5):
            ycopy(b, n).wait_recv()
        for c in block_chunks(b):
            cols = slice(c * W, (c + 1) * W)
            total = own[c] + r_p[c].astype(F32) + r_m[c].astype(F32)
            out[:, cols] = (total / (ve[:, cols] - pb[...])).astype(BF16)

    r = lax.broadcasted_iota(jnp.int32, (256, 256), 0)
    s = lax.broadcasted_iota(jnp.int32, (256, 256), 1)
    target = (r & 15) * 16 + ((r >> 4) & 7) * 2 + (r >> 7)
    perm[...] = jnp.where(s == target, 1.0, 0.0).astype(BF16)
    for cp in small:
        cp.wait()
    for t in range(2):
        line = mask[t:t + 1, :].astype(F32)
        mb[t] = jnp.broadcast_to(line, (128, pairs)).T
    pb[...] = jnp.broadcast_to(pe[...], (128, rows)).T

    own_copy.wait()
    for q in range(parts):
        relayout(q)
        stages(PRE[q])

    for b in range(NB):
        compute(b, PLAN[b])
        if b >= LAG:
            combine(b - LAG)
        if b >= LAG2:
            final(b - LAG2)
    for b in range(NB - LAG, NB):
        combine(b)
    for b in range(NB - LAG2, NB):
        final(b)

    for g in range(NG):
        for d in first_zd(g):
            first_z(g, d).wait_send()
        for d in (1, 2, 3):
            first_x(g, d).wait_send()
        first_partner(g).wait_send()
    for f in range(len(FIRST)):
        for d in range(1, ZN):
            for t in range(2):
                p_first(f, d, t).wait_send()
        p_partner_first(f).wait_send()

    @pl.loop(0, NP)
    def _(c):
        for n in range(4):
            p_x(c, n).wait_send()
            p_partner(c, n).wait_send()

    @pl.when(k == 0)
    def _():
        for g in range(NG):
            for cp in rows_all(g) + [row_partner(g, d) for d in range(ZN)]:
                cp.wait_send()

    @pl.when(k == 1)
    def _():
        for g in range(NG):
            for cp in cols_all(g) + [col_partner(g, d) for d in range(XN)]:
                cp.wait_send()

    for b in range(NB):
        for n in range(6):
            ycopy(b, n).wait_send()


def on_device(amplitudes, tile_mask, integrals, pair_energy, virt_energy):
    pairs, tiles, kdim = amplitudes.shape
    depth, ab = integrals.shape[1:]
    rows = pairs // YN
    half = rows // 2
    chunks = ab // W
    kt = kdim // 128
    amp = amplitudes.reshape(pairs, tiles, kt, 128).transpose(0, 2, 1, 3).reshape(pairs * kt * tiles, 128)
    vmem = pl.BlockSpec(memory_space=pltpu.VMEM)
    dma = pltpu.SemaphoreType.DMA
    return pl.pallas_call(
        kernel,
        out_shape=pltpu.VMEM((rows, ab), BF16),
        in_specs=[pl.BlockSpec(memory_space=pltpu.HBM)] * 5,
        out_specs=vmem,
        scratch_shapes=[
            pltpu.VMEM((tiles, pairs), jnp.int32),
            pltpu.VMEM((1, rows), F32),
            pltpu.VMEM((1, ab), F32),
            pltpu.VMEM(amp.shape, BF16),
            pltpu.VMEM((pairs, tiles * kdim), BF16),
            pltpu.VMEM((chunks, tiles, depth, W), BF16),
            pltpu.VMEM((chunks, tiles, XN, ZN, KN, depth, W), BF16),
            pltpu.VMEM((256, 256), BF16),
            pltpu.VMEM((tiles, pairs, 128), F32),
            pltpu.VMEM((rows, 128), F32),
            pltpu.VMEM((chunks, rows, W), BF16),
            pltpu.VMEM((chunks, rows, W), BF16),
            pltpu.VMEM((chunks, rows, W), BF16),
            pltpu.VMEM((chunks, half, W), BF16),
            pltpu.VMEM((chunks, half, W), BF16),
            pltpu.VMEM((chunks, rows, W), BF16),
            pltpu.VMEM((chunks, rows, W), BF16),
            pltpu.VMEM((chunks, half, W), F32),
            pltpu.VMEM((chunks, half, W), F32),
            pltpu.VMEM((chunks, rows, W), F32),
            dma((4,)),
            dma((chunks,)),
            dma((3,)),
            dma,
            dma((len(FIRST), ZN, KN)),
            dma((len(FIRST), ZN, KN)),
            dma((NP, 4)),
            dma((NP, 4)),
            dma((NP, 4)),
            dma((NP, 4)),
            dma((NG, 12)),
            dma((NG, ZN, KN)),
            dma((NG, 11)),
            dma((NG, 11)),
            dma((NG, ZN)),
            dma((NG, ZN)),
            dma((NB, 6)),
            dma((NB, 6)),
        ],
        compiler_params=pltpu.CompilerParams(collective_id=0, has_side_effects=True),
        name="ladder",
    )(amp, tile_mask.T, integrals, pair_energy[None, :], virt_energy[None, :])


def solution(mesh):
    placed = (
        P("pair", "virt", None),
        P("pair", "virt"),
        P("virt", "pair", None),
        P(("pair", "virt")),
        P(),
    )
    return jax.shard_map(
        on_device, mesh=mesh, in_specs=placed, out_specs=P(("pair", "virt"), None), check_vma=False
    )
```
